32 devices in a mesh: dp: 4 (over y, x), ctx: 8 (over z, core).
Axes of the slice: x: 2, y: 2, z: 4, core: 2. Of those that a mesh axis runs over, the one named last changes fastest.
Arguments:
- block_input: bfloat16 [4, 2048, 768], P('dp', 'ctx'), may hold values from -6 to 6
- doc_ids: int32 [4, 2048], P('dp', 'ctx'), may hold values from 0 to 7, never falling along the last dimension, each value on 1 to 1536 neighbouring positions
- out_grad: bfloat16 [4, 2048, 768], P('dp', 'ctx'), may hold values from -6 to 6
- ln1_gain: bfloat16 [2, 768], P(None, ('dp', 'ctx')), may hold values from 0.5 to 1.5
- ln1_bias: bfloat16 [2, 768], P(None, ('dp', 'ctx')), may hold values from -3 to 3
- w_qkv: bfloat16 [2, 768, 2304], P(None, ('dp', 'ctx')), may hold values from -0.21875 to 0.21875
- b_query: bfloat16 [2, 768], P(None, ('dp', 'ctx')), may hold values from -3 to 3
- b_value: bfloat16 [2, 768], P(None, ('dp', 'ctx')), may hold values from -3 to 3
- w_out: bfloat16 [2, 768, 768], P(None, ('dp', 'ctx')), may hold values from -0.875 to 0.875
- b_out: bfloat16 [2, 768], P(None, ('dp', 'ctx')), may hold values from -3 to 3
- ln2_gain: bfloat16 [2, 768], P(None, ('dp', 'ctx')), may hold values from 0.5 to 1.5
- ln2_bias: bfloat16 [2, 768], P(None, ('dp', 'ctx')), may hold values from -3 to 3
- w_fc: bfloat16 [2, 768, 3072], P(None, ('dp', 'ctx')), may hold values from -0.21875 to 0.21875
- b_fc: bfloat16 [2, 3072], P(None, ('dp', 'ctx')), may hold values from -3 to 3
- w_proj: bfloat16 [2, 3072, 768], P(None, ('dp', 'ctx')), may hold values from -0.109375 to 0.109375
- b_proj: bfloat16 [2, 768], P(None, ('dp', 'ctx')), may hold values from -3 to 3
Outputs:
- block_output: bfloat16 [4, 2048, 768], P('dp', 'ctx')
- grad_input: bfloat16 [4, 2048, 768], P('dp', 'ctx')
- grad_ln1_gain: float32 [2, 768], P(None, ('dp', 'ctx'))
- grad_ln1_bias: float32 [2, 768], P(None, ('dp', 'ctx'))
- grad_w_qkv: float32 [2, 768, 2304], P(None, ('dp', 'ctx'))
- grad_b_query: float32 [2, 768], P(None, ('dp', 'ctx'))
- grad_b_value: float32 [2, 768], P(None, ('dp', 'ctx'))
- grad_w_out: float32 [2, 768, 768], P(None, ('dp', 'ctx'))
- grad_b_out: float32 [2, 768], P(None, ('dp', 'ctx'))
- grad_ln2_gain: float32 [2, 768], P(None, ('dp', 'ctx'))
- grad_ln2_bias: float32 [2, 768], P(None, ('dp', 'ctx'))
- grad_w_fc: float32 [2, 768, 3072], P(None, ('dp', 'ctx'))
- grad_b_fc: float32 [2, 3072], P(None, ('dp', 'ctx'))
- grad_w_proj: float32 [2, 3072, 768], P(None, ('dp', 'ctx'))
- grad_b_proj: float32 [2, 768], P(None, ('dp', 'ctx'))
The draws below stay inside these ranges and needn't reach their ends.
Inputs may be any that keep to these rules, and one draw needn't show every extreme that they name: `doc_ids`: along each sequence the document numbers never fall; a document covers 1 to 1536 positions, and one covers exactly 1536.
All inputs are finite; a program needn't handle non-finite values.
Results may differ from the reference program's by a relative error of at most 0.03.
Values may be sent and summed in bfloat16 or wider, within the bound.
A program may use at most 256 MiB of HBM per device.

```python
import math
import jax
import jax.numpy as jnp
import numpy as np
from jax import lax

D = 768
HEADS = 12
HEAD = 64
FF = 3072
LAYERS = 2
SEQ_LEN = 2048
SEQS = 4
DOCS = 8
DOC_MOST = 1536


def block_scale(rng, shape, pieces, least, high):
    def one(dim, parts):
        steps = jax.random.uniform(jax.random.fold_in(jax.random.fold_in(rng, 6), dim), (parts,), jnp.float32, least / len(pieces), high / len(pieces))
        return jnp.repeat(jnp.exp(steps), shape[dim] // parts).reshape((-1,) + (1,) * (len(shape) - dim - 1))

    level = one(*pieces[0])
    for cut in pieces[1:]:
        level = level * one(*cut)
    return level


def profile(number_of, total, most, slope):
    loads = [(1 << 20) // math.isqrt(grade ** slope) + 1 for grade in range(2, number_of + 1)]
    rest, counts = total - most - (number_of - 1), [1] * (number_of - 1)
    while rest > 0:
        movable = [i for i in range(number_of - 1) if counts[i] < most]
        mass, budget = sum([loads[i] for i in movable]), rest
        for i in movable:
            extra = min(most - counts[i], max(1, budget * loads[i] // mass), rest)
            counts[i] = counts[i] + extra
            rest = rest - extra
    return np.array([most] + counts)


def uneven(stream_key, count, total, limit, lean):
    if count == 2:
        one = jax.random.randint(stream_key, (), max(1, total - limit), min(limit, total - 1) + 1)
        return jnp.stack([one, total - one])
    sizes = jnp.asarray(profile(count, total, limit, lean), jnp.int32)
    pairs = (count - 1) // 2
    donor, receiver = sizes[1:1 + 2 * pairs:2], sizes[2:2 + 2 * pairs:2]
    slack = jnp.minimum(donor - 1, limit - receiver)
    moved = jax.random.randint(jax.random.fold_in(stream_key, 1), (pairs,), 0, 1 << 20) % (slack + 1)
    sizes = sizes.at[1:1 + 2 * pairs:2].set(donor - moved).at[2:2 + 2 * pairs:2].set(receiver + moved)
    return sizes[jax.random.permutation(jax.random.fold_in(stream_key, 2), count)]


def gaussian(stream_key, extent, deviation, limit, shards=(), kind=jnp.bfloat16):
    drawn = jax.random.normal(stream_key, extent, jnp.float32) * deviation
    if len(shards) > 0:
        drawn = block_scale(stream_key, extent, shards, -0.22, 0.18) * drawn
    return jnp.clip(drawn, min=-limit, max=limit).astype(kind)


def setup_inputs(seed: int = 0) -> dict:
    arg_keys = jax.random.split(jax.random.key(seed), 17)
    block_input = gaussian(arg_keys[0], (SEQS, SEQ_LEN, D), 1.0, 6.0, ((0, 4), (1, 8)))
    doc_ids = jax.vmap(lambda own: jnp.searchsorted(jnp.cumsum(uneven(own, DOCS, SEQ_LEN, DOC_MOST, 2)), jnp.arange(SEQ_LEN), side="right"))(jax.random.split(arg_keys[1], SEQS)).reshape((SEQS, SEQ_LEN)).astype(jnp.int32)
    out_grad = gaussian(arg_keys[2], (SEQS, SEQ_LEN, D), 1.0, 6.0, ((0, 4), (1, 8)))
    ln1_gain = jnp.clip(1.0 + 0.1 * jax.random.normal(arg_keys[3], (LAYERS, D), jnp.float32), 0.5, 1.5).astype(jnp.bfloat16)
    ln1_bias = gaussian(arg_keys[4], (LAYERS, D), 0.3, 3.0, ((1, 32),))
    w_qkv = gaussian(arg_keys[5], (LAYERS, D, 3 * D), D ** -0.5, 0.21875, ((1, 32),))
    b_query = gaussian(arg_keys[6], (LAYERS, D), 0.5, 3.0, ((1, 32),))
    b_value = gaussian(arg_keys[7], (LAYERS, D), 0.5, 3.0, ((1, 32),))
    w_out = gaussian(arg_keys[8], (LAYERS, D, D), (D // 16) ** -0.5, 0.875, ((1, 32),))
    b_out = gaussian(arg_keys[9], (LAYERS, D), 0.3, 3.0, ((1, 32),))
    ln2_gain = jnp.clip(1.0 + 0.1 * jax.random.normal(arg_keys[10], (LAYERS, D), jnp.float32), 0.5, 1.5).astype(jnp.bfloat16)
    ln2_bias = gaussian(arg_keys[11], (LAYERS, D), 0.3, 3.0, ((1, 32),))
    w_fc = gaussian(arg_keys[12], (LAYERS, D, FF), D ** -0.5, 0.21875, ((1, 32),))
    b_fc = gaussian(arg_keys[13], (LAYERS, FF), 0.5, 3.0, ((1, 32),))
    w_proj = gaussian(arg_keys[14], (LAYERS, FF, D), FF ** -0.5, 0.109375, ((1, 32),))
    b_proj = gaussian(arg_keys[15], (LAYERS, D), 0.3, 3.0, ((1, 32),))
    return {"block_input": block_input, "doc_ids": doc_ids, "out_grad": out_grad, "ln1_gain": ln1_gain, "ln1_bias": ln1_bias, "w_qkv": w_qkv, "b_query": b_query, "b_value": b_value, "w_out": w_out, "b_out": b_out, "ln2_gain": ln2_gain, "ln2_bias": ln2_bias, "w_fc": w_fc, "b_fc": b_fc, "w_proj": w_proj, "b_proj": b_proj}


norm_eps = 1e-05
masked_value = -1e+30
gelu_coeff = 0.7978845608028654
cubic_coeff = 0.044715
query_block = 512

def widen(narrow):
    return lax.optimization_barrier(narrow).astype(jnp.float32)

def layer_norm(residual, norm_gain, norm_bias):
    row_mean = lax.optimization_barrier(jnp.mean(residual, axis=-1, keepdims=True))
    centered = residual - row_mean
    variance = lax.optimization_barrier(jnp.mean(centered * centered, axis=-1, keepdims=True))
    inv_std = lax.rsqrt(variance + norm_eps)
    normed = centered * inv_std
    return (normed * norm_gain + norm_bias, normed, inv_std)

def norm_back(grad_norm, normed, inv_std, norm_gain):
    scaled = grad_norm * norm_gain
    return inv_std * (scaled - lax.optimization_barrier(jnp.mean(scaled, axis=-1, keepdims=True)) - normed * lax.optimization_barrier(jnp.mean(scaled * normed, axis=-1, keepdims=True)))

def gelu_value(values_in):
    inner_arg = gelu_coeff * (values_in + cubic_coeff * values_in * values_in * values_in)
    return 0.5 * values_in * (1.0 + jnp.tanh(inner_arg))

def gelu_slope(values_in):
    tanh_val = jnp.tanh(gelu_coeff * (values_in + cubic_coeff * values_in * values_in * values_in))
    return 0.5 * (1.0 + tanh_val) + 0.5 * values_in * (1.0 - tanh_val * tanh_val) * gelu_coeff * (1.0 + 3.0 * cubic_coeff * values_in * values_in)

def forward_layer(residual, layer_params, attend_fwd):
    norm1_gain, norm1_bias, qkv_weight, query_bias, value_bias, out_weight, out_bias, norm2_gain, norm2_bias, fc_weight, fc_bias, proj_weight, proj_bias = layer_params
    model_width = residual.shape[1]
    normed_in, normed1, inv_std1 = layer_norm(residual, norm1_gain.astype(jnp.float32), norm1_bias.astype(jnp.float32))
    attn_in = normed_in.astype(jnp.bfloat16)
    projected = jnp.dot(attn_in, qkv_weight, preferred_element_type=jnp.float32)
    queries = (projected[:, :model_width] + query_bias.astype(jnp.float32)).astype(jnp.bfloat16)
    keys = projected[:, model_width:2 * model_width].astype(jnp.bfloat16)
    values = (projected[:, 2 * model_width:] + value_bias.astype(jnp.float32)).astype(jnp.bfloat16)
    mixed_rows, log_total = attend_fwd(queries, keys, values)
    middle = residual + jnp.dot(mixed_rows, out_weight, preferred_element_type=jnp.float32) + out_bias.astype(jnp.float32)
    normed_mid, normed2, inv_std2 = layer_norm(middle, norm2_gain.astype(jnp.float32), norm2_bias.astype(jnp.float32))
    ffn_in = normed_mid.astype(jnp.bfloat16)
    pre_act = jnp.dot(ffn_in, fc_weight, preferred_element_type=jnp.float32) + fc_bias.astype(jnp.float32)
    hidden = gelu_value(pre_act).astype(jnp.bfloat16)
    result = middle + jnp.dot(hidden, proj_weight, preferred_element_type=jnp.float32) + proj_bias.astype(jnp.float32)
    return (result, (normed1, inv_std1, attn_in, queries, keys, values, mixed_rows, log_total, normed2, inv_std2, ffn_in, pre_act, hidden))

def backward_layer(grad_residual, saved_rows, layer_params, attend_back):
    normed1, inv_std1, attn_in, queries, keys, values, mixed_rows, log_total, normed2, inv_std2, ffn_in, pre_act, hidden = saved_rows
    norm1_gain, norm1_bias, qkv_weight, query_bias, value_bias, out_weight, out_bias, norm2_gain, norm2_bias, fc_weight, fc_bias, proj_weight, proj_bias = layer_params
    grad_narrow = grad_residual.astype(jnp.bfloat16)
    grad_proj_w = jnp.dot(hidden.T, grad_narrow, preferred_element_type=jnp.float32)
    grad_proj_b = lax.optimization_barrier(jnp.sum(grad_residual, axis=0))
    grad_hidden = jnp.dot(grad_narrow, proj_weight.T, preferred_element_type=jnp.float32)
    grad_pre = grad_hidden * gelu_slope(pre_act)
    pre_narrow = grad_pre.astype(jnp.bfloat16)
    grad_fc_w = jnp.dot(ffn_in.T, pre_narrow, preferred_element_type=jnp.float32)
    grad_fc_b = lax.optimization_barrier(jnp.sum(grad_pre, axis=0))
    grad_norm2 = jnp.dot(pre_narrow, fc_weight.T, preferred_element_type=jnp.float32)
    grad_gain2 = lax.optimization_barrier(jnp.sum(grad_norm2 * normed2, axis=0))
    grad_bias2 = lax.optimization_barrier(jnp.sum(grad_norm2, axis=0))
    grad_middle = grad_residual + norm_back(grad_norm2, normed2, inv_std2, norm2_gain.astype(jnp.float32))
    middle_narrow = grad_middle.astype(jnp.bfloat16)
    grad_out_w = jnp.dot(mixed_rows.T, middle_narrow, preferred_element_type=jnp.float32)
    grad_out_b = lax.optimization_barrier(jnp.sum(grad_middle, axis=0))
    grad_mixed = jnp.dot(middle_narrow, out_weight.T, preferred_element_type=jnp.float32).astype(jnp.bfloat16)
    grad_queries, grad_keys, grad_values = attend_back(queries, keys, values, mixed_rows, grad_mixed, log_total)
    proj_narrow = jnp.concatenate([grad_queries, grad_keys, grad_values], axis=1).astype(jnp.bfloat16)
    grad_qkv_w = jnp.dot(attn_in.T, proj_narrow, preferred_element_type=jnp.float32)
    grad_query_b = lax.optimization_barrier(jnp.sum(grad_queries, axis=0))
    grad_value_b = lax.optimization_barrier(jnp.sum(grad_values, axis=0))
    grad_norm1 = jnp.dot(proj_narrow, qkv_weight.T, preferred_element_type=jnp.float32)
    grad_gain1 = lax.optimization_barrier(jnp.sum(grad_norm1 * normed1, axis=0))
    grad_bias1 = lax.optimization_barrier(jnp.sum(grad_norm1, axis=0))
    grad_before = grad_middle + norm_back(grad_norm1, normed1, inv_std1, norm1_gain.astype(jnp.float32))
    return (grad_before, (grad_gain1, grad_bias1, grad_qkv_w, grad_query_b, grad_value_b, grad_out_w, grad_out_b, grad_gain2, grad_bias2, grad_fc_w, grad_fc_b, grad_proj_w, grad_proj_b))

def seq_mask(query_pos, query_ids, positions, doc_row):
    return ((doc_row[None, :] == query_ids[:, None]) & (positions[None, :] <= query_pos[:, None]))[None]

def attention_forward(queries, keys, values, doc_row):
    seq_length = queries.shape[0]
    block_count = seq_length // query_block
    positions = jnp.arange(seq_length, dtype=jnp.int32)
    score_scale = HEAD ** (-0.5)
    key_wide = widen(keys).reshape(seq_length, HEADS, HEAD)
    value_wide = widen(values).reshape(seq_length, HEADS, HEAD)

    def one_block(block_args):
        query_rows, query_pos, query_ids = block_args
        scores = jnp.einsum('qhd,khd->hqk', widen(query_rows), key_wide) * score_scale
        allowed = seq_mask(query_pos, query_ids, positions, doc_row)
        scores = jnp.where(allowed, scores, masked_value)
        row_max = lax.optimization_barrier(jnp.max(scores, axis=-1))
        weights = jnp.where(allowed, jnp.exp(scores - row_max[..., None]), 0.0)
        weight_sum = lax.optimization_barrier(jnp.sum(weights, axis=-1))
        mixed_heads = jnp.einsum('hqk,khd->qhd', widen(weights.astype(jnp.bfloat16)), value_wide) / jnp.transpose(weight_sum)[..., None]
        return (mixed_heads.astype(jnp.bfloat16), row_max + jnp.log(weight_sum))
    mixed_heads, log_total = lax.map(one_block, (queries.reshape(block_count, query_block, HEADS, HEAD), positions.reshape(block_count, query_block), doc_row.reshape(block_count, query_block)))
    return (mixed_heads.reshape(seq_length, HEADS * HEAD), log_total)

def attention_backward(queries, keys, values, mixed_rows, grad_mixed, log_total, doc_row):
    seq_length = queries.shape[0]
    block_count = seq_length // query_block
    positions = jnp.arange(seq_length, dtype=jnp.int32)
    score_scale = HEAD ** (-0.5)
    key_wide = widen(keys).reshape(seq_length, HEADS, HEAD)
    value_wide = widen(values).reshape(seq_length, HEADS, HEAD)
    query_wide = widen(queries).reshape(seq_length, HEADS, HEAD)
    grad_wide = widen(grad_mixed).reshape(seq_length, HEADS, HEAD)
    row_delta = lax.optimization_barrier(jnp.sum(grad_wide * widen(mixed_rows).reshape(seq_length, HEADS, HEAD), axis=-1))

    def one_block(running, block_args):
        grad_keys, grad_values = running
        query_rows, grad_rows, lse_rows, delta_rows, query_pos, query_ids = block_args
        scores = jnp.einsum('qhd,khd->hqk', query_rows, key_wide) * score_scale
        allowed = seq_mask(query_pos, query_ids, positions, doc_row)
        scores = jnp.where(allowed, scores, masked_value)
        probabilities = jnp.where(allowed, jnp.exp(scores - lse_rows[..., None]), 0.0)
        grad_probs = jnp.einsum('qhd,khd->hqk', grad_rows, value_wide)
        grad_scores = probabilities * (grad_probs - jnp.transpose(delta_rows)[..., None])
        grad_narrow = widen(grad_scores.astype(jnp.bfloat16))
        prob_narrow = widen(probabilities.astype(jnp.bfloat16))
        grad_queries = jnp.einsum('hqk,khd->qhd', grad_narrow, key_wide) * score_scale
        grad_keys = grad_keys + jnp.einsum('hqk,qhd->khd', grad_narrow, query_rows) * score_scale
        grad_values = grad_values + jnp.einsum('hqk,qhd->khd', prob_narrow, grad_rows)
        return ((grad_keys, grad_values), grad_queries)
    zero_grads = jnp.zeros((seq_length, HEADS, HEAD), jnp.float32)
    (grad_keys, grad_values), grad_queries = lax.scan(one_block, (zero_grads, zero_grads), (query_wide.reshape(block_count, query_block, HEADS, HEAD), grad_wide.reshape(block_count, query_block, HEADS, HEAD), log_total, row_delta.reshape(block_count, query_block, HEADS), positions.reshape(block_count, query_block), doc_row.reshape(block_count, query_block)))
    model_width = HEADS * HEAD
    return (grad_queries.reshape(seq_length, model_width), grad_keys.reshape(seq_length, model_width), grad_values.reshape(seq_length, model_width))

def reference(block_input, doc_ids, out_grad, ln1_gain, ln1_bias, w_qkv, b_query, b_value, w_out, b_out, ln2_gain, ln2_bias, w_fc, b_fc, w_proj, b_proj):
    all_params = (ln1_gain, ln1_bias, w_qkv, b_query, b_value, w_out, b_out, ln2_gain, ln2_bias, w_fc, b_fc, w_proj, b_proj)

    def one_sequence(grad_sums, seq_args):
        input_rows, doc_row, cot_rows = seq_args

        def attend_fwd(queries, keys, values):
            return attention_forward(queries, keys, values, doc_row)

        def attend_back(queries, keys, values, mixed_rows, grad_mixed, log_total):
            return attention_backward(queries, keys, values, mixed_rows, grad_mixed, log_total, doc_row)
        residual = input_rows.astype(jnp.float32)
        saved_list = []
        for layer_idx in range(LAYERS):
            layer_params = tuple((param[layer_idx] for param in all_params))
            residual, saved_rows = forward_layer(residual, layer_params, attend_fwd)
            saved_list.append(saved_rows)
        output_rows = residual.astype(jnp.bfloat16)
        grad_residual = cot_rows.astype(jnp.float32)
        new_sums = list(grad_sums)
        for layer_idx in reversed(range(LAYERS)):
            layer_params = tuple((param[layer_idx] for param in all_params))
            grad_residual, layer_grads = backward_layer(grad_residual, saved_list[layer_idx], layer_params, attend_back)
            new_sums = [total_grad.at[layer_idx].add(part_grad) for total_grad, part_grad in zip(new_sums, layer_grads)]
        return (tuple(new_sums), (output_rows, grad_residual.astype(jnp.bfloat16)))
    initial = tuple((jnp.zeros(param.shape, jnp.float32) for param in all_params))
    grad_sums, (block_output, grad_input) = lax.scan(one_sequence, initial, (block_input, doc_ids, out_grad))
    return (block_output, grad_input, grad_sums[0], grad_sums[1], grad_sums[2], grad_sums[3], grad_sums[4], grad_sums[5], grad_sums[6], grad_sums[7], grad_sums[8], grad_sums[9], grad_sums[10], grad_sums[11], grad_sums[12])
```

```python
import functools

import jax
import jax.numpy as jnp
from jax import lax
from jax.experimental import pallas as pl
from jax.experimental.pallas import tpu as pltpu
from jax.sharding import PartitionSpec as P

HEAD = 64
LAYERS = 2


norm_eps = 1e-05
masked_value = -1e30
gelu_coeff = 0.7978845608028654
cubic_coeff = 0.044715
key_block = 512

def swap(value, dp_bits, ctx_bits):
    dp_size, ctx_size = lax.axis_size("dp"), lax.axis_size("ctx")
    pairs = [
        (i, ((i // ctx_size) ^ dp_bits) * ctx_size + ((i % ctx_size) ^ ctx_bits))
        for i in range(dp_size * ctx_size)
    ]
    return lax.ppermute(value, ("dp", "ctx"), pairs)


def place_kernel(dp_size, chips, *refs):
    pieces, whole, held, in_sem, out_sem = refs[: 2 * dp_size], *refs[2 * dp_size :]
    half = held.shape[-1]
    dp_rank, ctx_rank = lax.axis_index("dp"), lax.axis_index("ctx")
    chip, core = ctx_rank // 2, ctx_rank % 2
    arrivals = []
    for n, piece in enumerate(pieces):
        for k in range(chips):
            copy = pltpu.make_async_copy(piece.at[k], held.at[n, k], in_sem.at[n, k])
            copy.start()
            arrivals.append((n, k, copy))
    leaving = []
    for n, k, copy in arrivals:
        copy.wait()
        side, move = n // dp_size, n % dp_size
        row = (dp_rank ^ move) * chips + (chip ^ k)
        column = pl.multiple_of((core ^ side) * half, half)
        out = pltpu.make_async_copy(
            held.at[n, k], whole.at[row, :, pl.ds(column, half)], out_sem.at[n, k]
        )
        out.start()
        leaving.append(out)
    for out in leaving:
        out.wait()


def gather_rows(shard, order):
    dp_size, chips = lax.axis_size("dp"), lax.axis_size("ctx") // 2
    rows, columns = shard.shape
    half = columns // 2
    core = lax.axis_index("ctx") % 2
    kept = lax.dynamic_slice_in_dim(shard, core * half, half, 1)
    given = lax.dynamic_slice_in_dim(shard, (1 - core) * half, half, 1)
    got = swap(given, 0, 1)
    own = jnp.where(core == 0, jnp.concatenate([kept, got]), jnp.concatenate([got, kept]))
    line = jnp.stack([own] + [swap(own, 0, 2 * k) for k in range(1, chips)])
    pieces = {0: line}
    for bit in order:
        for place in list(pieces):
            pieces[place ^ bit] = swap(pieces[place], bit, 0)
    near = [pieces[place] for place in range(dp_size)]
    far = [swap(piece, 0, 1) for piece in near]
    whole = pl.pallas_call(
        functools.partial(place_kernel, dp_size, chips),
        out_shape=jax.ShapeDtypeStruct((dp_size * chips, 2 * rows, columns), shard.dtype),
        in_specs=[pl.BlockSpec(memory_space=pl.ANY)] * (2 * dp_size),
        out_specs=pl.BlockSpec(memory_space=pl.ANY),
        scratch_shapes=[
            pltpu.VMEM((2 * dp_size, chips, 2 * rows, half), shard.dtype),
            pltpu.SemaphoreType.DMA((2 * dp_size, chips)),
            pltpu.SemaphoreType.DMA((2 * dp_size, chips)),
        ],
        cost_estimate=pl.CostEstimate(
            flops=0, transcendentals=0, bytes_accessed=4 * dp_size * chips * rows * columns * 2
        ),
    )(*near, *far)
    return whole.reshape(dp_size * chips * 2 * rows, columns)


def pick(value, place, axis):
    return lax.dynamic_index_in_dim(value, place, axis, keepdims=False)


def reduce_rows(left, right, order):
    dp_size, chips = lax.axis_size("dp"), lax.axis_size("ctx") // 2
    dp_rank, ctx_rank = lax.axis_index("dp"), lax.axis_index("ctx")
    chip, core = ctx_rank // 2, ctx_rank % 2
    rows, columns = left.shape[1] // (dp_size * chips * 2), right.shape[1]
    half = columns // 2
    own_side = lax.dynamic_slice_in_dim(right, core * half, half, 1)
    far_side = lax.dynamic_slice_in_dim(right, (1 - core) * half, half, 1)
    far = jnp.dot(left.T, far_side, preferred_element_type=jnp.float32).astype(jnp.bfloat16)
    got = swap(far, 0, 1)
    part = (
        jnp.dot(left.T, own_side, preferred_element_type=jnp.float32) + got.astype(jnp.float32)
    ).astype(jnp.bfloat16)
    bits = [1 << n for n in reversed(range(dp_size.bit_length() - 1))]
    part = part.reshape([2] * len(bits) + [chips, 2 * rows, half])
    for bit in order:
        axis = bits.index(bit)
        bits.remove(bit)
        side = (dp_rank // bit) % 2
        got = swap(pick(part, 1 - side, axis), bit, 0)
        part = (pick(part, side, axis).astype(jnp.float32) + got.astype(jnp.float32)).astype(
            jnp.bfloat16
        )
    total = pick(part, chip, 0).astype(jnp.float32)
    for k in range(1, chips):
        total = total + swap(pick(part, chip ^ k, 0), 0, 2 * k).astype(jnp.float32)
    total = total.reshape(2, rows, half)
    got = swap(pick(total, 1 - core, 0), 0, 1)
    kept = pick(total, core, 0)
    return jnp.where(
        core == 0,
        jnp.concatenate([kept, got], axis=1),
        jnp.concatenate([got, kept], axis=1),
    )


def gather_small(packed):
    dp_size, ctx_size = lax.axis_size("dp"), lax.axis_size("ctx")
    mine = lax.axis_index("dp") * ctx_size + lax.axis_index("ctx")
    held = packed.reshape(1, 8, -1)
    held = jnp.concatenate([held] + [swap(held, 0, k) for k in range(1, ctx_size)])
    bit = 1
    while bit < dp_size:
        held = jnp.concatenate([held, swap(held, bit, 0)])
        bit *= 2
    devices = dp_size * ctx_size
    held = held.reshape(devices, -1)
    source = mine ^ jnp.arange(devices, dtype=jnp.int32)
    chosen = (source[:, None] == jnp.arange(devices, dtype=jnp.int32)[None, :]).astype(held.dtype)
    return jnp.dot(chosen, held, preferred_element_type=jnp.float32).astype(held.dtype)


def reduce_small(terms):
    dp_size, ctx_size = lax.axis_size("dp"), lax.axis_size("ctx")
    dp_rank, ctx_rank = lax.axis_index("dp"), lax.axis_index("ctx")
    width = terms.shape[1]
    part = terms.reshape(dp_size, ctx_size, 8, width // 8)
    total = pick(part, dp_rank, 0)
    for k in range(1, dp_size):
        total = total + swap(pick(part, dp_rank ^ k, 0), k, 0)
    row = pick(total, ctx_rank, 0)
    for k in range(1, ctx_size):
        row = row + swap(pick(total, ctx_rank ^ k, 0), 0, k)
    return row.reshape(width)


def layer_norm(residual, norm_gain, norm_bias):
    row_mean = jnp.mean(residual, axis=-1, keepdims=True)
    centered = residual - row_mean
    variance = jnp.mean(centered * centered, axis=-1, keepdims=True)
    inv_std = lax.rsqrt(variance + norm_eps)
    normed = centered * inv_std
    return (normed * norm_gain + norm_bias, normed, inv_std)


def norm_back(grad_norm, normed, inv_std, norm_gain):
    scaled = grad_norm * norm_gain
    return inv_std * (
        scaled
        - jnp.mean(scaled, axis=-1, keepdims=True)
        - normed * jnp.mean(scaled * normed, axis=-1, keepdims=True)
    )


def gelu_value(values_in):
    inner_arg = gelu_coeff * (values_in + cubic_coeff * values_in * values_in * values_in)
    return 0.5 * values_in * (1.0 + jnp.tanh(inner_arg))


def gelu_slope(values_in):
    tanh_val = jnp.tanh(gelu_coeff * (values_in + cubic_coeff * values_in * values_in * values_in))
    return 0.5 * (1.0 + tanh_val) + 0.5 * values_in * (1.0 - tanh_val * tanh_val) * gelu_coeff * (
        1.0 + 3.0 * cubic_coeff * values_in * values_in
    )


def forward_layer(residual, layer_params, attend_fwd):
    (
        norm1_gain,
        norm1_bias,
        qkv_weight,
        query_bias,
        value_bias,
        out_weight,
        out_bias,
        norm2_gain,
        norm2_bias,
        fc_weight,
        fc_bias,
        proj_weight,
        proj_bias,
    ) = layer_params
    model_width = residual.shape[1]
    normed_in, normed1, inv_std1 = layer_norm(
        residual, norm1_gain.astype(jnp.float32), norm1_bias.astype(jnp.float32)
    )
    attn_in = normed_in.astype(jnp.bfloat16)
    projected = jnp.dot(attn_in, qkv_weight, preferred_element_type=jnp.float32)
    queries = (projected[:, :model_width] + query_bias.astype(jnp.float32)).astype(jnp.bfloat16)
    keys = projected[:, model_width : 2 * model_width].astype(jnp.bfloat16)
    values = (projected[:, 2 * model_width :] + value_bias.astype(jnp.float32)).astype(jnp.bfloat16)
    mixed_rows, log_total = attend_fwd(queries, keys, values)
    middle = (
        residual
        + jnp.dot(mixed_rows, out_weight, preferred_element_type=jnp.float32)
        + out_bias.astype(jnp.float32)
    )
    normed_mid, normed2, inv_std2 = layer_norm(
        middle, norm2_gain.astype(jnp.float32), norm2_bias.astype(jnp.float32)
    )
    ffn_in = normed_mid.astype(jnp.bfloat16)
    pre_act = jnp.dot(ffn_in, fc_weight, preferred_element_type=jnp.float32) + fc_bias.astype(
        jnp.float32
    )
    hidden = gelu_value(pre_act).astype(jnp.bfloat16)
    result = (
        middle
        + jnp.dot(hidden, proj_weight, preferred_element_type=jnp.float32)
        + proj_bias.astype(jnp.float32)
    )
    return (
        result,
        (
            normed1,
            inv_std1,
            attn_in,
            queries,
            keys,
            values,
            mixed_rows,
            log_total,
            normed2,
            inv_std2,
            ffn_in,
            pre_act,
            hidden,
        ),
    )


def backward_layer(grad_residual, saved_rows, layer_params, attend_back, orders):
    (
        normed1,
        inv_std1,
        attn_in,
        queries,
        keys,
        values,
        mixed_rows,
        log_total,
        normed2,
        inv_std2,
        ffn_in,
        pre_act,
        hidden,
    ) = saved_rows
    (
        norm1_gain,
        norm1_bias,
        qkv_weight,
        query_bias,
        value_bias,
        out_weight,
        out_bias,
        norm2_gain,
        norm2_bias,
        fc_weight,
        fc_bias,
        proj_weight,
        proj_bias,
    ) = layer_params
    grad_narrow = grad_residual.astype(jnp.bfloat16)
    grad_proj_w = reduce_rows(hidden, grad_narrow, orders[2])
    grad_proj_b = jnp.sum(grad_residual, axis=0)
    grad_hidden = jnp.dot(grad_narrow, proj_weight.T, preferred_element_type=jnp.float32)
    grad_pre = grad_hidden * gelu_slope(pre_act)
    pre_narrow = grad_pre.astype(jnp.bfloat16)
    grad_fc_w = reduce_rows(ffn_in, pre_narrow, orders[1])
    grad_fc_b = jnp.sum(grad_pre, axis=0)
    grad_norm2 = jnp.dot(pre_narrow, fc_weight.T, preferred_element_type=jnp.float32)
    grad_gain2 = jnp.sum(grad_norm2 * normed2, axis=0)
    grad_bias2 = jnp.sum(grad_norm2, axis=0)
    grad_middle = grad_residual + norm_back(
        grad_norm2, normed2, inv_std2, norm2_gain.astype(jnp.float32)
    )
    middle_narrow = grad_middle.astype(jnp.bfloat16)
    grad_out_w = reduce_rows(mixed_rows, middle_narrow, orders[1])
    grad_out_b = jnp.sum(grad_middle, axis=0)
    grad_mixed = jnp.dot(middle_narrow, out_weight.T, preferred_element_type=jnp.float32).astype(
        jnp.bfloat16
    )
    grad_queries, grad_keys, grad_values = attend_back(
        queries, keys, values, mixed_rows, grad_mixed, log_total
    )
    proj_narrow = jnp.concatenate([grad_queries, grad_keys, grad_values], axis=1).astype(
        jnp.bfloat16
    )
    grad_qkv_w = reduce_rows(attn_in, proj_narrow, orders[0])
    grad_query_b = jnp.sum(grad_queries, axis=0)
    grad_value_b = jnp.sum(grad_values, axis=0)
    grad_norm1 = jnp.dot(proj_narrow, qkv_weight.T, preferred_element_type=jnp.float32)
    grad_gain1 = jnp.sum(grad_norm1 * normed1, axis=0)
    grad_bias1 = jnp.sum(grad_norm1, axis=0)
    grad_before = grad_middle + norm_back(
        grad_norm1, normed1, inv_std1, norm1_gain.astype(jnp.float32)
    )
    return (
        grad_before,
        (
            grad_gain1,
            grad_bias1,
            grad_qkv_w,
            grad_query_b,
            grad_value_b,
            grad_out_w,
            grad_out_b,
            grad_gain2,
            grad_bias2,
            grad_fc_w,
            grad_fc_b,
            grad_proj_w,
            grad_proj_b,
        ),
    )


def visible(key_ids, key_places, query_ids, query_places):
    same_doc = key_ids[:, None, :] == query_ids[:, :, None]
    causal = key_places[None, :] <= query_places[:, None]
    return (same_doc & causal[None])[:, None]


def shards(
    block_input,
    doc_ids,
    out_grad,
    ln1_gain,
    ln1_bias,
    w_qkv,
    b_query,
    b_value,
    w_out,
    b_out,
    ln2_gain,
    ln2_bias,
    w_fc,
    b_fc,
    w_proj,
    b_proj,
):
    seq_count, local_len, model_width = block_input.shape
    head_count = model_width // HEAD
    row_count = seq_count * local_len
    score_scale = HEAD ** (-0.5)
    ctx_rank = lax.axis_index("ctx")
    all_ids = lax.all_gather(doc_ids, "ctx", axis=1, tiled=True)
    seq_length = all_ids.shape[1]
    query_pos = ctx_rank * local_len + jnp.arange(local_len, dtype=jnp.int32)

    def split_heads(three_dim):
        return three_dim.reshape(three_dim.shape[0], three_dim.shape[1], head_count, HEAD)

    def as_seqs(flat_rows):
        return flat_rows.reshape(seq_count, local_len, model_width)

    def attend_fwd(queries, keys, values):
        query_heads = split_heads(as_seqs(queries))
        running_max = jnp.full((seq_count, head_count, local_len), masked_value, jnp.float32)
        key_piece = lax.all_gather(as_seqs(keys), "ctx", axis=1, tiled=True)
        value_piece = lax.all_gather(as_seqs(values), "ctx", axis=1, tiled=True)
        piece_len = key_piece.shape[1]
        key_heads = split_heads(key_piece)
        value_heads = split_heads(value_piece)
        key_places = jnp.arange(piece_len, dtype=jnp.int32)
        allowed = visible(all_ids, key_places, doc_ids, query_pos)
        scores = (
            jnp.einsum(
                "sqhd,skhd->shqk", query_heads, key_heads, preferred_element_type=jnp.float32
            )
            * score_scale
        )
        scores = jnp.where(allowed, scores, masked_value)
        new_max = jnp.maximum(running_max, jnp.max(scores, axis=-1))
        weights = jnp.where(allowed, jnp.exp(scores - new_max[..., None]), 0.0)
        weight_sum = jnp.sum(weights, axis=-1)
        accumulated = jnp.einsum(
            "shqk,skhd->shqd",
            weights.astype(jnp.bfloat16),
            value_heads,
            preferred_element_type=jnp.float32,
        )
        running_max, weight_sum, accumulated = (new_max, weight_sum, accumulated)
        mixed_heads = accumulated / weight_sum[..., None]
        mixed_rows = (
            jnp.transpose(mixed_heads, (0, 2, 1, 3))
            .reshape(row_count, model_width)
            .astype(jnp.bfloat16)
        )
        return (mixed_rows, running_max + jnp.log(weight_sum))

    def attend_back(queries, keys, values, mixed_rows, grad_mixed, log_total):
        query_rows = as_seqs(queries)
        grad_rows = as_seqs(grad_mixed)
        query_heads = split_heads(query_rows)
        grad_heads = split_heads(grad_rows)
        row_delta = jnp.transpose(
            jnp.sum(
                grad_heads.astype(jnp.float32)
                * split_heads(as_seqs(mixed_rows)).astype(jnp.float32),
                axis=-1,
            ),
            (0, 2, 1),
        )
        key_all, value_all = (
            lax.all_gather(as_seqs(keys), "ctx", axis=1, tiled=True),
            lax.all_gather(as_seqs(values), "ctx", axis=1, tiled=True),
        )
        block_count = seq_length // key_block

        def block_terms(offset):
            key_heads = split_heads(lax.dynamic_slice_in_dim(key_all, offset, key_block, 1))
            value_heads = split_heads(lax.dynamic_slice_in_dim(value_all, offset, key_block, 1))
            key_ids = lax.dynamic_slice_in_dim(all_ids, offset, key_block, 1)
            key_places = offset + jnp.arange(key_block, dtype=jnp.int32)
            allowed = visible(key_ids, key_places, doc_ids, query_pos)
            scores = (
                jnp.einsum(
                    "sqhd,skhd->shqk", query_heads, key_heads, preferred_element_type=jnp.float32
                )
                * score_scale
            )
            scores = jnp.where(allowed, scores, masked_value)
            probabilities = jnp.where(allowed, jnp.exp(scores - log_total[..., None]), 0.0)
            grad_probs = jnp.einsum(
                "sqhd,skhd->shqk", grad_heads, value_heads, preferred_element_type=jnp.float32
            )
            grad_narrow = (probabilities * (grad_probs - row_delta[..., None])).astype(jnp.bfloat16)
            grad_queries = (
                jnp.einsum(
                    "shqk,skhd->sqhd", grad_narrow, key_heads, preferred_element_type=jnp.float32
                )
                * score_scale
            )
            return (probabilities, grad_narrow, grad_queries)

        zero_query = jnp.zeros((seq_count, local_len, head_count, HEAD), jnp.float32)

        def full_step(block_index, running):
            grad_q, grad_k, grad_v = running
            offset = block_index * key_block
            probabilities, grad_narrow, grad_queries = block_terms(offset)
            part_keys = (
                jnp.einsum(
                    "shqk,sqhd->skhd", grad_narrow, query_heads, preferred_element_type=jnp.float32
                )
                * score_scale
            ).reshape(seq_count, key_block, model_width)
            part_values = jnp.einsum(
                "shqk,sqhd->skhd",
                probabilities.astype(jnp.bfloat16),
                grad_heads,
                preferred_element_type=jnp.float32,
            ).reshape(seq_count, key_block, model_width)
            grad_k = lax.dynamic_update_slice_in_dim(grad_k, part_keys, offset, 1)
            grad_v = lax.dynamic_update_slice_in_dim(grad_v, part_values, offset, 1)
            return (grad_q + grad_queries, grad_k, grad_v)

        zero_keys = jnp.zeros((seq_count, seq_length, model_width), jnp.float32)
        grad_q, grad_k, grad_v = lax.fori_loop(
            0, block_count, full_step, (zero_query, zero_keys, zero_keys)
        )
        grad_k, grad_v = (
            lax.psum_scatter(
                grad_k.astype(jnp.bfloat16), "ctx", scatter_dimension=1, tiled=True
            ).astype(jnp.float32),
            lax.psum_scatter(
                grad_v.astype(jnp.bfloat16), "ctx", scatter_dimension=1, tiled=True
            ).astype(jnp.float32),
        )
        return (
            grad_q.reshape(row_count, model_width),
            grad_k.reshape(row_count, model_width),
            grad_v.reshape(row_count, model_width),
        )

    dp_size, ctx_size = lax.axis_size("dp"), lax.axis_size("ctx")
    devices = dp_size * ctx_size
    rising = [1 << n for n in range(dp_size.bit_length() - 1)]
    falling = rising[::-1]
    narrow_list = (ln1_gain, ln1_bias, b_query, b_value, b_out, ln2_gain, ln2_bias, b_proj)
    narrow_count = LAYERS * len(narrow_list)
    slot = narrow_list[0].shape[1]
    fc_slot = b_fc.shape[1]
    used = narrow_count * slot + LAYERS * fc_slot
    packed_size = -(-used // 1024) * 1024
    packed = jnp.concatenate(
        [jnp.stack(narrow_list, 1).reshape(-1), b_fc.reshape(-1)]
        + [jnp.zeros((packed_size - used,), jnp.bfloat16)]
    )
    small = gather_small(packed)
    narrow_all = jnp.transpose(
        small[:, : narrow_count * slot].reshape(devices, narrow_count, slot), (1, 0, 2)
    ).reshape(LAYERS, len(narrow_list), devices * slot)
    fc_all = jnp.transpose(
        small[:, narrow_count * slot : used].reshape(devices, LAYERS, fc_slot), (1, 0, 2)
    ).reshape(LAYERS, devices * fc_slot)

    residual = block_input.reshape(row_count, model_width).astype(jnp.float32)
    kept_params = []
    saved_list = []
    for layer_idx in range(LAYERS):
        ways = (rising, falling) if layer_idx % 2 == 0 else (falling, rising)
        first = gather_rows(
            jnp.concatenate([w_qkv[layer_idx], w_out[layer_idx]], axis=1), ways[0]
        )
        fc_weight = gather_rows(w_fc[layer_idx], ways[1])
        proj_weight = gather_rows(w_proj[layer_idx], ways[0])
        narrow = narrow_all[layer_idx]
        layer_params = (
            narrow[0],
            narrow[1],
            first[:, : 3 * model_width],
            narrow[2],
            narrow[3],
            first[:, 3 * model_width :],
            narrow[4],
            narrow[5],
            narrow[6],
            fc_weight,
            fc_all[layer_idx],
            proj_weight,
            narrow[7],
        )
        residual, saved_rows = forward_layer(residual, layer_params, attend_fwd)
        kept_params.append(layer_params)
        saved_list.append(saved_rows)
    output_rows = residual.astype(jnp.bfloat16).reshape(seq_count, local_len, model_width)
    grad_residual = out_grad.reshape(row_count, model_width).astype(jnp.float32)
    reduced = [None] * LAYERS
    for layer_idx in reversed(range(LAYERS)):
        orders = (rising, falling, rising) if layer_idx % 2 == 0 else (falling, rising, falling)
        grad_residual, reduced[layer_idx] = backward_layer(
            grad_residual, saved_list[layer_idx], kept_params[layer_idx], attend_back, orders
        )
    grad_rows = grad_residual.astype(jnp.bfloat16).reshape(seq_count, local_len, model_width)
    narrow_members = (0, 1, 3, 4, 6, 7, 8, 12)
    narrow_terms = jnp.stack([grads[member] for grads in reduced for member in narrow_members])
    fc_terms = jnp.stack([grads[10] for grads in reduced])
    terms = jnp.concatenate(
        [
            jnp.transpose(narrow_terms.reshape(narrow_count, devices, slot), (1, 0, 2)).reshape(
                devices, -1
            ),
            jnp.transpose(fc_terms.reshape(LAYERS, devices, fc_slot), (1, 0, 2)).reshape(
                devices, -1
            ),
            jnp.zeros((devices, packed_size - used), jnp.float32),
        ],
        axis=1,
    )
    sums = reduce_small(terms)
    narrow_sums = sums[: narrow_count * slot].reshape(LAYERS, len(narrow_list), slot)
    fc_sums = sums[narrow_count * slot : used].reshape(LAYERS, fc_slot)
    stacked = []
    for member in range(13):
        if member in narrow_members:
            stacked.append(narrow_sums[:, narrow_members.index(member)])
        elif member == 10:
            stacked.append(fc_sums)
        else:
            stacked.append(jnp.stack([grads[member] for grads in reduced]))
    return (output_rows, grad_rows, *stacked)


def solution(mesh):
    return jax.shard_map(
        shards,
        mesh=mesh,
        in_specs=(
            P("dp", "ctx", None),
            P("dp", "ctx"),
            P("dp", "ctx", None),
            P(None, ("dp", "ctx")),
            P(None, ("dp", "ctx")),
            P(None, ("dp", "ctx"), None),
            P(None, ("dp", "ctx")),
            P(None, ("dp", "ctx")),
            P(None, ("dp", "ctx"), None),
            P(None, ("dp", "ctx")),
            P(None, ("dp", "ctx")),
            P(None, ("dp", "ctx")),
            P(None, ("dp", "ctx"), None),
            P(None, ("dp", "ctx")),
            P(None, ("dp", "ctx"), None),
            P(None, ("dp", "ctx")),
        ),
        out_specs=(
            P("dp", "ctx", None),
            P("dp", "ctx", None),
            P(None, ("dp", "ctx")),
            P(None, ("dp", "ctx")),
            P(None, ("dp", "ctx"), None),
            P(None, ("dp", "ctx")),
            P(None, ("dp", "ctx")),
            P(None, ("dp", "ctx"), None),
            P(None, ("dp", "ctx")),
            P(None, ("dp", "ctx")),
            P(None, ("dp", "ctx")),
            P(None, ("dp", "ctx"), None),
            P(None, ("dp", "ctx")),
            P(None, ("dp", "ctx"), None),
            P(None, ("dp", "ctx")),
        ),
        check_vma=False,
    )
```

```python
import functools
import math

import jax
import jax.numpy as jnp
from jax import lax
from jax.experimental import pallas as pl
from jax.experimental.pallas import tpu as pltpu
from jax.sharding import PartitionSpec as P

HEAD = 64
LAYERS = 2
DOCS = 8


norm_eps = 1e-05
masked_value = -1e30
gelu_coeff = 0.7978845608028654
cubic_coeff = 0.044715

def swap(value, dp_bits, ctx_bits):
    dp_size, ctx_size = lax.axis_size("dp"), lax.axis_size("ctx")
    pairs = [
        (i, ((i // ctx_size) ^ dp_bits) * ctx_size + ((i % ctx_size) ^ ctx_bits))
        for i in range(dp_size * ctx_size)
    ]
    return lax.ppermute(value, ("dp", "ctx"), pairs)


def place_kernel(dp_size, chips, *refs):
    pieces, whole, held, in_sem, out_sem = refs[: 2 * dp_size], *refs[2 * dp_size :]
    half = held.shape[-1]
    dp_rank, ctx_rank = lax.axis_index("dp"), lax.axis_index("ctx")
    chip, core = ctx_rank // 2, ctx_rank % 2
    arrivals = []
    for n, piece in enumerate(pieces):
        for k in range(chips):
            copy = pltpu.make_async_copy(piece.at[k], held.at[n, k], in_sem.at[n, k])
            copy.start()
            arrivals.append((n, k, copy))
    leaving = []
    for n, k, copy in arrivals:
        copy.wait()
        side, move = n // dp_size, n % dp_size
        row = (dp_rank ^ move) * chips + (chip ^ k)
        column = pl.multiple_of((core ^ side) * half, half)
        out = pltpu.make_async_copy(
            held.at[n, k], whole.at[row, :, pl.ds(column, half)], out_sem.at[n, k]
        )
        out.start()
        leaving.append(out)
    for out in leaving:
        out.wait()


def gather_rows(shard, order):
    dp_size, chips = lax.axis_size("dp"), lax.axis_size("ctx") // 2
    rows, columns = shard.shape
    half = columns // 2
    core = lax.axis_index("ctx") % 2
    kept = lax.dynamic_slice_in_dim(shard, core * half, half, 1)
    given = lax.dynamic_slice_in_dim(shard, (1 - core) * half, half, 1)
    got = swap(given, 0, 1)
    own = jnp.where(core == 0, jnp.concatenate([kept, got]), jnp.concatenate([got, kept]))
    line = jnp.stack([own] + [swap(own, 0, 2 * k) for k in range(1, chips)])
    pieces = {0: line}
    for bit in order:
        for place in list(pieces):
            pieces[place ^ bit] = swap(pieces[place], bit, 0)
    near = [pieces[place] for place in range(dp_size)]
    far = [swap(piece, 0, 1) for piece in near]
    whole = pl.pallas_call(
        functools.partial(place_kernel, dp_size, chips),
        out_shape=jax.ShapeDtypeStruct((dp_size * chips, 2 * rows, columns), shard.dtype),
        in_specs=[pl.BlockSpec(memory_space=pl.ANY)] * (2 * dp_size),
        out_specs=pl.BlockSpec(memory_space=pl.ANY),
        scratch_shapes=[
            pltpu.VMEM((2 * dp_size, chips, 2 * rows, half), shard.dtype),
            pltpu.SemaphoreType.DMA((2 * dp_size, chips)),
            pltpu.SemaphoreType.DMA((2 * dp_size, chips)),
        ],
        cost_estimate=pl.CostEstimate(
            flops=0, transcendentals=0, bytes_accessed=4 * dp_size * chips * rows * columns * 2
        ),
    )(*near, *far)
    return whole.reshape(dp_size * chips * 2 * rows, columns)


def pick(value, place, axis):
    return lax.dynamic_index_in_dim(value, place, axis, keepdims=False)


def reduce_rows(left, right, order, left_dim=0, right_dim=0):
    dp_size, chips = lax.axis_size("dp"), lax.axis_size("ctx") // 2
    dp_rank, ctx_rank = lax.axis_index("dp"), lax.axis_index("ctx")
    chip, core = ctx_rank // 2, ctx_rank % 2
    rows = left.shape[1 - left_dim] // (dp_size * chips * 2)
    columns = right.shape[1 - right_dim]
    half = columns // 2
    own_side = lax.dynamic_slice_in_dim(right, core * half, half, 1 - right_dim)
    far_side = lax.dynamic_slice_in_dim(right, (1 - core) * half, half, 1 - right_dim)
    got = swap(contract(left, far_side, left_dim, right_dim).astype(jnp.bfloat16), 0, 1)
    part = (contract(left, own_side, left_dim, right_dim) + got.astype(jnp.float32)).astype(
        jnp.bfloat16
    )
    bits = [1 << n for n in reversed(range(dp_size.bit_length() - 1))]
    part = part.reshape([2] * len(bits) + [chips, 2 * rows, half])
    for bit in order:
        axis = bits.index(bit)
        bits.remove(bit)
        side = (dp_rank // bit) % 2
        got = swap(pick(part, 1 - side, axis), bit, 0)
        part = (pick(part, side, axis).astype(jnp.float32) + got.astype(jnp.float32)).astype(
            jnp.bfloat16
        )
    total = pick(part, chip, 0).astype(jnp.float32)
    for k in range(1, chips):
        total = total + swap(pick(part, chip ^ k, 0), 0, 2 * k).astype(jnp.float32)
    total = total.reshape(2, rows, half)
    got = swap(pick(total, 1 - core, 0), 0, 1)
    kept = pick(total, core, 0)
    return jnp.where(
        core == 0,
        jnp.concatenate([kept, got], axis=1),
        jnp.concatenate([got, kept], axis=1),
    )


def gather_small(packed):
    dp_size, ctx_size = lax.axis_size("dp"), lax.axis_size("ctx")
    mine = lax.axis_index("dp") * ctx_size + lax.axis_index("ctx")
    held = packed.reshape(1, 8, -1)
    held = jnp.concatenate([held] + [swap(held, 0, k) for k in range(1, ctx_size)])
    bit = 1
    while bit < dp_size:
        held = jnp.concatenate([held, swap(held, bit, 0)])
        bit *= 2
    devices = dp_size * ctx_size
    held = held.reshape(devices, -1)
    source = mine ^ jnp.arange(devices, dtype=jnp.int32)
    chosen = (source[:, None] == jnp.arange(devices, dtype=jnp.int32)[None, :]).astype(held.dtype)
    return jnp.dot(chosen, held, preferred_element_type=jnp.float32).astype(held.dtype)


def reduce_small(terms):
    dp_size, ctx_size = lax.axis_size("dp"), lax.axis_size("ctx")
    dp_rank, ctx_rank = lax.axis_index("dp"), lax.axis_index("ctx")
    width = terms.shape[1]
    part = terms.reshape(dp_size, ctx_size, 8, width // 8)
    total = pick(part, dp_rank, 0)
    for k in range(1, dp_size):
        total = total + swap(pick(part, dp_rank ^ k, 0), k, 0)
    row = pick(total, ctx_rank, 0)
    for k in range(1, ctx_size):
        row = row + swap(pick(total, ctx_rank ^ k, 0), 0, k)
    return row.reshape(width)


def layer_norm(residual, norm_gain, norm_bias):
    row_mean = jnp.mean(residual, axis=-1, keepdims=True)
    centered = residual - row_mean
    variance = jnp.mean(centered * centered, axis=-1, keepdims=True)
    inv_std = lax.rsqrt(variance + norm_eps)
    normed = centered * inv_std
    return (normed * norm_gain + norm_bias, normed, inv_std)


def norm_back(grad_norm, normed, inv_std, norm_gain):
    scaled = grad_norm * norm_gain
    return inv_std * (
        scaled
        - jnp.mean(scaled, axis=-1, keepdims=True)
        - normed * jnp.mean(scaled * normed, axis=-1, keepdims=True)
    )


def gelu_value(values_in):
    inner_arg = gelu_coeff * (values_in + cubic_coeff * values_in * values_in * values_in)
    return 0.5 * values_in * (1.0 + jnp.tanh(inner_arg))


def gelu_slope(values_in):
    tanh_val = jnp.tanh(gelu_coeff * (values_in + cubic_coeff * values_in * values_in * values_in))
    return 0.5 * (1.0 + tanh_val) + 0.5 * values_in * (1.0 - tanh_val * tanh_val) * gelu_coeff * (
        1.0 + 3.0 * cubic_coeff * values_in * values_in
    )


def fetch(pairs):
    copies = [pltpu.make_async_copy(*pair) for pair in pairs]
    for copy in copies:
        copy.start()
    for copy in copies:
        copy.wait()


def contract(left, right, left_dim, right_dim):
    return lax.dot_general(
        left, right, (((left_dim,), (right_dim,)), ((), ())), preferred_element_type=jnp.float32
    )


def allowed_keys(key_chunk, starts, length, own):
    places = lax.broadcasted_iota(jnp.int32, (length, length), 0)
    allowed = places + key_chunk * length >= starts
    if own:
        allowed &= places <= lax.broadcasted_iota(jnp.int32, (length, length), 1)
    return allowed


def mix_kernel(parts, shares, *refs):
    first_ref, starts_ref = refs[:2]
    mine, theirs = refs[2 : 2 + parts], refs[2 + parts]
    out_ref, log_ref, queries, both, total, sems = refs[3 + parts :]
    width, length = out_ref.shape[1:]
    ctx_rank = lax.axis_index("ctx")
    part, share = ctx_rank // shares, ctx_rank % shares
    pairs = []
    for k in range(parts):
        chunk = (part ^ k) * shares
        pairs.append((mine[k].at[pl.ds(0, width)], queries.at[k], sems.at[k, 0]))
        pairs.append(
            (mine[k].at[pl.ds(width, 2 * width)], both.at[chunk + share], sems.at[k, 1])
        )
        for j in range(1, shares):
            pairs.append((theirs.at[j - 1, k], both.at[chunk + (share ^ j)], sems.at[k, 1 + j]))
    fetch(pairs)
    heads = width // HEAD

    def one_chunk(k, carry):
        chunk = (part ^ k) * shares + share
        starts = starts_ref[chunk]
        total[...] = jnp.zeros_like(total)

        def block(key_chunk, state, own):
            allowed = allowed_keys(key_chunk, starts, length, own)
            following = []
            for head in range(heads):
                top, weight = state[head]
                rows = slice(head * HEAD, (head + 1) * HEAD)
                value_rows = slice(width + head * HEAD, width + (head + 1) * HEAD)
                score = contract(both[key_chunk, rows], queries[k, rows], 0, 0)
                score = jnp.where(allowed, score, masked_value)
                new_top = jnp.maximum(top, jnp.max(score, axis=0, keepdims=True))
                prob = jnp.exp(score - new_top)
                shrink = jnp.exp(top - new_top)
                weight = weight * shrink + jnp.sum(prob, axis=0, keepdims=True)
                total[rows] = total[rows] * shrink + contract(
                    both[key_chunk, value_rows], prob.astype(jnp.bfloat16), 1, 0
                )
                following.append((new_top, weight))
            return tuple(following)

        empty = (
            jnp.full((1, length), masked_value, jnp.float32),
            jnp.zeros((1, length), jnp.float32),
        )
        state = lax.fori_loop(
            first_ref[chunk], chunk, lambda at, s: block(at, s, False), (empty,) * heads
        )
        state = block(chunk, state, True)
        for head in range(heads):
            top, weight = state[head]
            rows = slice(head * HEAD, (head + 1) * HEAD)
            out_ref[k, rows] = (total[rows] / weight).astype(out_ref.dtype)
            log_ref[k, head : head + 1] = top + jnp.log(weight)
        return carry

    lax.fori_loop(0, parts, one_chunk, 0)


def mix_back_kernel(parts, shares, *refs):
    first_ref, starts_ref, mixed, log_ref = refs[:4]
    mine, grads, theirs = refs[4 : 4 + parts], refs[4 + parts : 4 + 2 * parts], refs[4 + 2 * parts]
    out_ref, own_ref, far_ref, queries, both, slopes, totals, sems = refs[5 + 2 * parts :]
    width, length = out_ref.shape[1:]
    ctx_rank = lax.axis_index("ctx")
    part, share = ctx_rank // shares, ctx_rank % shares
    pairs = []
    for k in range(parts):
        chunk = (part ^ k) * shares
        pairs.append((mine[k].at[pl.ds(0, width)], queries.at[k], sems.at[k, 0]))
        pairs.append((grads[k], slopes.at[k], sems.at[k, 1]))
        pairs.append(
            (mine[k].at[pl.ds(width, 2 * width)], both.at[chunk + share], sems.at[k, 2])
        )
        for j in range(1, shares):
            pairs.append((theirs.at[j - 1, k], both.at[chunk + (share ^ j)], sems.at[k, 2 + j]))
    fetch(pairs)
    totals[...] = jnp.zeros_like(totals)
    heads = width // HEAD

    def one_chunk(k, carry):
        chunk = (part ^ k) * shares + share
        starts = starts_ref[chunk]
        deltas, logs = [], []
        for head in range(heads):
            rows = slice(head * HEAD, (head + 1) * HEAD)
            deltas.append(
                jnp.sum(
                    slopes[k, rows].astype(jnp.float32) * mixed[k, rows].astype(jnp.float32),
                    axis=0,
                    keepdims=True,
                )
            )
            logs.append(log_ref[k, head : head + 1])

        def block(key_chunk, state, own):
            allowed = allowed_keys(key_chunk, starts, length, own)
            following = []
            for head in range(heads):
                rows = slice(head * HEAD, (head + 1) * HEAD)
                value_rows = slice(width + head * HEAD, width + (head + 1) * HEAD)
                keys, values = both[key_chunk, rows], both[key_chunk, value_rows]
                asked, slope = queries[k, rows], slopes[k, rows]
                score = contract(keys, asked, 0, 0)
                prob = jnp.exp(jnp.where(allowed, score - logs[head], masked_value))
                grad_prob = contract(values, slope, 0, 0)
                grad_score = (prob * (grad_prob - deltas[head])).astype(jnp.bfloat16)
                totals[key_chunk, value_rows] += contract(slope, prob.astype(jnp.bfloat16), 1, 1)
                totals[key_chunk, rows] += contract(asked, grad_score, 1, 1)
                following.append(state[head] + contract(keys, grad_score, 1, 0))
            return tuple(following)

        zero = jnp.zeros((HEAD, length), jnp.float32)
        state = lax.fori_loop(
            first_ref[chunk], chunk, lambda at, s: block(at, s, False), (zero,) * heads
        )
        state = block(chunk, state, True)
        for head in range(heads):
            rows = slice(head * HEAD, (head + 1) * HEAD)
            out_ref[k, rows] = (state[head] * HEAD ** (-0.5)).astype(out_ref.dtype)
        return carry

    lax.fori_loop(0, parts, one_chunk, 0)
    for k in range(parts):
        chunk = (part ^ k) * shares
        own_ref[k] = totals[chunk + share]
        for j in range(1, shares):
            far_ref[j - 1, k] = totals[chunk + (share ^ j)].astype(far_ref.dtype)


def spread(grouped, parts, shares):
    part = lax.axis_index("ctx") // shares
    return [
        pick(grouped, part ^ k, 0) if k == 0 else swap(pick(grouped, part ^ k, 0), 0, shares * k)
        for k in range(parts)
    ]


def collect(pieces, parts, shares):
    part = lax.axis_index("ctx") // shares
    held = jnp.stack([p if k == 0 else swap(p, 0, shares * k) for k, p in enumerate(pieces)])
    return jnp.concatenate([pick(held, part ^ j, 0) for j in range(parts)])


def attend(grouped, starts, first, parts, shares):
    width, length = grouped.shape[1] // 3, grouped.shape[2]
    mine = spread(grouped, parts, shares)
    joint = jnp.stack([piece[width:] for piece in mine])
    theirs = jnp.stack([swap(joint, 0, j) for j in range(1, shares)])
    mixed, logs = pl.pallas_call(
        functools.partial(mix_kernel, parts, shares),
        out_shape=(
            jax.ShapeDtypeStruct((parts, width, length), jnp.bfloat16),
            jax.ShapeDtypeStruct((parts, 8, length), jnp.float32),
        ),
        in_specs=[
            pl.BlockSpec(memory_space=pltpu.SMEM),
            pl.BlockSpec(memory_space=pltpu.VMEM),
        ]
        + [pl.BlockSpec(memory_space=pl.ANY)] * (parts + 1),
        out_specs=(pl.BlockSpec(memory_space=pltpu.VMEM),) * 2,
        scratch_shapes=[
            pltpu.VMEM((parts, width, length), jnp.bfloat16),
            pltpu.VMEM((parts * shares, 2 * width, length), jnp.bfloat16),
            pltpu.VMEM((width, length), jnp.float32),
            pltpu.SemaphoreType.DMA((parts, 1 + shares)),
        ],
        cost_estimate=pl.CostEstimate(
            flops=2 * parts * parts * shares * length * length * width * 2,
            transcendentals=0,
            bytes_accessed=4 * parts * width * length * 2,
        ),
    )(first, starts, *mine, theirs)
    return mixed, logs, mine, theirs


def attend_back(grouped_grads, kept, starts, first, parts, shares):
    mixed, logs, mine, theirs = kept
    width, length = mixed.shape[1:]
    grads = spread(grouped_grads, parts, shares)
    grad_queries, own, far = pl.pallas_call(
        functools.partial(mix_back_kernel, parts, shares),
        out_shape=(
            jax.ShapeDtypeStruct((parts, width, length), jnp.bfloat16),
            jax.ShapeDtypeStruct((parts, 2 * width, length), jnp.float32),
            jax.ShapeDtypeStruct((shares - 1, parts, 2 * width, length), jnp.bfloat16),
        ),
        in_specs=[
            pl.BlockSpec(memory_space=pltpu.SMEM),
            pl.BlockSpec(memory_space=pltpu.VMEM),
            pl.BlockSpec(memory_space=pltpu.VMEM),
            pl.BlockSpec(memory_space=pltpu.VMEM),
        ]
        + [pl.BlockSpec(memory_space=pl.ANY)] * (2 * parts + 1),
        out_specs=(pl.BlockSpec(memory_space=pltpu.VMEM),) * 3,
        scratch_shapes=[
            pltpu.VMEM((parts, width, length), jnp.bfloat16),
            pltpu.VMEM((parts * shares, 2 * width, length), jnp.bfloat16),
            pltpu.VMEM((parts, width, length), jnp.bfloat16),
            pltpu.VMEM((parts * shares, 2 * width, length), jnp.float32),
            pltpu.SemaphoreType.DMA((parts, 2 + shares)),
        ],
        cost_estimate=pl.CostEstimate(
            flops=5 * parts * parts * shares * length * length * width * 2,
            transcendentals=0,
            bytes_accessed=8 * parts * width * length * 2,
        ),
    )(first, starts, mixed, logs, *mine, *grads, theirs)
    for j in range(1, shares):
        own = own + swap(far[j - 1], 0, j).astype(jnp.float32)
    joint = jnp.concatenate([grad_queries, own.astype(jnp.bfloat16)], axis=1)
    return collect([joint[k] for k in range(parts)], parts, shares)


def forward_layer(residual, layer_params, plan):
    (
        norm1_gain,
        norm1_bias,
        qkv_weight,
        qkv_bias,
        qkv_scale,
        out_weight,
        out_bias,
        norm2_gain,
        norm2_bias,
        fc_weight,
        fc_bias,
        proj_weight,
        proj_bias,
    ) = layer_params
    starts, first, parts, shares = plan
    normed_in, normed1, inv_std1 = layer_norm(residual, norm1_gain, norm1_bias)
    attn_in = normed_in.astype(jnp.bfloat16)
    projected = (contract(qkv_weight, attn_in, 0, 1) + qkv_bias[:, None]) * qkv_scale[:, None]
    grouped = projected.astype(jnp.bfloat16).reshape(parts, -1, residual.shape[0])
    kept = attend(grouped, starts, first, parts, shares)
    mixed_columns = collect([kept[0][k] for k in range(parts)], parts, shares)
    middle = residual + contract(mixed_columns, out_weight, 0, 0) + out_bias
    normed_mid, normed2, inv_std2 = layer_norm(middle, norm2_gain, norm2_bias)
    ffn_in = normed_mid.astype(jnp.bfloat16)
    pre_act = jnp.dot(ffn_in, fc_weight, preferred_element_type=jnp.float32) + fc_bias
    hidden = gelu_value(pre_act).astype(jnp.bfloat16)
    result = middle + jnp.dot(hidden, proj_weight, preferred_element_type=jnp.float32) + proj_bias
    return (
        result,
        (
            normed1,
            inv_std1,
            attn_in,
            kept,
            mixed_columns,
            normed2,
            inv_std2,
            ffn_in,
            pre_act,
            hidden,
        ),
    )


def backward_layer(grad_residual, saved_rows, layer_params, plan, orders):
    (
        normed1,
        inv_std1,
        attn_in,
        kept,
        mixed_columns,
        normed2,
        inv_std2,
        ffn_in,
        pre_act,
        hidden,
    ) = saved_rows
    (
        norm1_gain,
        norm1_bias,
        qkv_weight,
        qkv_bias,
        qkv_scale,
        out_weight,
        out_bias,
        norm2_gain,
        norm2_bias,
        fc_weight,
        fc_bias,
        proj_weight,
        proj_bias,
    ) = layer_params
    starts, first, parts, shares = plan
    grad_narrow = grad_residual.astype(jnp.bfloat16)
    grad_proj_w = reduce_rows(hidden, grad_narrow, orders[2])
    grad_proj_b = jnp.sum(grad_residual, axis=0)
    grad_hidden = contract(grad_narrow, proj_weight, 1, 1)
    grad_pre = grad_hidden * gelu_slope(pre_act)
    pre_narrow = grad_pre.astype(jnp.bfloat16)
    grad_fc_w = reduce_rows(ffn_in, pre_narrow, orders[1])
    grad_fc_b = jnp.sum(grad_pre, axis=0)
    grad_norm2 = contract(pre_narrow, fc_weight, 1, 1)
    grad_gain2 = jnp.sum(grad_norm2 * normed2, axis=0)
    grad_bias2 = jnp.sum(grad_norm2, axis=0)
    grad_middle = grad_residual + norm_back(grad_norm2, normed2, inv_std2, norm2_gain)
    middle_narrow = grad_middle.astype(jnp.bfloat16)
    grad_out_w = reduce_rows(mixed_columns, middle_narrow, orders[1], left_dim=1)
    grad_out_b = jnp.sum(grad_middle, axis=0)
    grad_mixed = contract(out_weight, middle_narrow, 1, 1).astype(jnp.bfloat16)
    grad_mixed = grad_mixed.reshape(parts, -1, grad_mixed.shape[1])
    grad_qkv = attend_back(grad_mixed, kept, starts, first, parts, shares)
    grad_qkv_w = reduce_rows(attn_in, grad_qkv, orders[0], right_dim=1)
    grad_qkv_b = jnp.sum(grad_qkv.astype(jnp.float32), axis=1).reshape(parts, 3, -1)
    grad_norm1 = contract(grad_qkv, qkv_weight, 0, 1)
    grad_gain1 = jnp.sum(grad_norm1 * normed1, axis=0)
    grad_bias1 = jnp.sum(grad_norm1, axis=0)
    grad_before = grad_middle + norm_back(grad_norm1, normed1, inv_std1, norm1_gain)
    return (
        grad_before,
        (
            grad_gain1,
            grad_bias1,
            by_kind(grad_qkv_w, parts),
            grad_qkv_b[:, 0].reshape(-1),
            grad_qkv_b[:, 2].reshape(-1),
            grad_out_w,
            grad_out_b,
            grad_gain2,
            grad_bias2,
            grad_fc_w,
            grad_fc_b,
            grad_proj_w,
            grad_proj_b,
        ),
    )


def by_part(columns, parts):
    rows = columns.shape[0]
    return jnp.swapaxes(columns.reshape(rows, 3, parts, -1), 1, 2).reshape(rows, -1)


def by_kind(columns, parts):
    rows = columns.shape[0]
    return jnp.swapaxes(columns.reshape(rows, parts, 3, -1), 1, 2).reshape(rows, -1)


def shards(
    block_input,
    doc_ids,
    out_grad,
    ln1_gain,
    ln1_bias,
    w_qkv,
    b_query,
    b_value,
    w_out,
    b_out,
    ln2_gain,
    ln2_bias,
    w_fc,
    b_fc,
    w_proj,
    b_proj,
):
    seq_count, local_len, model_width = block_input.shape
    row_count = seq_count * local_len
    dp_size, ctx_size = lax.axis_size("dp"), lax.axis_size("ctx")
    devices = dp_size * ctx_size
    parts = math.gcd(model_width // HEAD, ctx_size)
    shares = ctx_size // parts
    rising = [1 << n for n in range(dp_size.bit_length() - 1)]
    falling = rising[::-1]
    narrow_list = (ln1_gain, ln1_bias, b_query, b_value, b_out, ln2_gain, ln2_bias, b_proj)
    narrow_count = LAYERS * len(narrow_list)
    slot = narrow_list[0].shape[1]
    fc_slot = b_fc.shape[1]
    used = narrow_count * slot + LAYERS * fc_slot
    packed_size = -(-(used + row_count) // 1024) * 1024
    packed = jnp.concatenate(
        [
            jnp.stack(narrow_list, 1).reshape(-1),
            b_fc.reshape(-1),
            doc_ids.reshape(-1).astype(jnp.bfloat16),
            jnp.zeros((packed_size - used - row_count,), jnp.bfloat16),
        ]
    )
    small = gather_small(packed)
    narrow_all = (
        jnp.transpose(
            small[:, : narrow_count * slot].reshape(devices, narrow_count, slot), (1, 0, 2)
        )
        .reshape(LAYERS, len(narrow_list), devices * slot)
        .astype(jnp.float32)
    )
    fc_all = (
        jnp.transpose(
            small[:, narrow_count * slot : used].reshape(devices, LAYERS, fc_slot), (1, 0, 2)
        )
        .reshape(LAYERS, devices * fc_slot)
        .astype(jnp.float32)
    )
    ids = pick(
        small[:, used : used + row_count].reshape(dp_size, ctx_size, row_count),
        lax.axis_index("dp"),
        0,
    )
    ids = lax.optimization_barrier(ids.astype(jnp.int32))
    starts = jnp.zeros((ctx_size, row_count), jnp.int32)
    for number in range(DOCS):
        before = jnp.sum((ids < number).astype(jnp.int32))
        starts = jnp.where(ids == number, before, starts)
    first = starts[:, 0] // row_count
    plan = (starts.reshape(ctx_size, 1, row_count), first, parts, shares)
    qkv_scale = jnp.tile(
        jnp.concatenate(
            [
                jnp.full((model_width // parts,), HEAD ** (-0.5), jnp.float32),
                jnp.ones((2 * model_width // parts,), jnp.float32),
            ]
        ),
        parts,
    )

    residual = block_input.reshape(row_count, model_width).astype(jnp.float32)
    kept_params = []
    saved_list = []
    for layer_idx in range(LAYERS):
        ways = (rising, falling) if layer_idx % 2 == 0 else (falling, rising)
        joined = gather_rows(
            jnp.concatenate([by_part(w_qkv[layer_idx], parts), w_out[layer_idx]], axis=1), ways[0]
        )
        fc_weight = gather_rows(w_fc[layer_idx], ways[1])
        proj_weight = gather_rows(w_proj[layer_idx], ways[0])
        narrow = narrow_all[layer_idx]
        qkv_bias = by_part(
            jnp.concatenate([narrow[2], jnp.zeros_like(narrow[2]), narrow[3]])[None], parts
        )[0]
        layer_params = (
            narrow[0],
            narrow[1],
            joined[:, : 3 * model_width],
            qkv_bias,
            qkv_scale,
            joined[:, 3 * model_width :],
            narrow[4],
            narrow[5],
            narrow[6],
            fc_weight,
            fc_all[layer_idx],
            proj_weight,
            narrow[7],
        )
        residual, saved_rows = forward_layer(residual, layer_params, plan)
        kept_params.append(layer_params)
        saved_list.append(saved_rows)
    output_rows = residual.astype(jnp.bfloat16).reshape(seq_count, local_len, model_width)
    grad_residual = out_grad.reshape(row_count, model_width).astype(jnp.float32)
    reduced = [None] * LAYERS
    for layer_idx in reversed(range(LAYERS)):
        orders = (rising, falling, rising) if layer_idx % 2 == 0 else (falling, rising, falling)
        grad_residual, reduced[layer_idx] = backward_layer(
            grad_residual, saved_list[layer_idx], kept_params[layer_idx], plan, orders
        )
    grad_rows = grad_residual.astype(jnp.bfloat16).reshape(seq_count, local_len, model_width)
    term_size = -(-used // 1024) * 1024
    narrow_members = (0, 1, 3, 4, 6, 7, 8, 12)
    narrow_terms = jnp.stack([grads[member] for grads in reduced for member in narrow_members])
    fc_terms = jnp.stack([grads[10] for grads in reduced])
    terms = jnp.concatenate(
        [
            jnp.transpose(narrow_terms.reshape(narrow_count, devices, slot), (1, 0, 2)).reshape(
                devices, -1
            ),
            jnp.transpose(fc_terms.reshape(LAYERS, devices, fc_slot), (1, 0, 2)).reshape(
                devices, -1
            ),
            jnp.zeros((devices, term_size - used), jnp.float32),
        ],
        axis=1,
    )
    sums = reduce_small(terms)
    narrow_sums = sums[: narrow_count * slot].reshape(LAYERS, len(narrow_list), slot)
    fc_sums = sums[narrow_count * slot : used].reshape(LAYERS, fc_slot)
    stacked = []
    for member in range(13):
        if member in narrow_members:
            stacked.append(narrow_sums[:, narrow_members.index(member)])
        elif member == 10:
            stacked.append(fc_sums)
        else:
            stacked.append(jnp.stack([grads[member] for grads in reduced]))
    return (output_rows, grad_rows, *stacked)


def solution(mesh):
    return jax.shard_map(
        shards,
        mesh=mesh,
        in_specs=(
            P("dp", "ctx", None),
            P("dp", "ctx"),
            P("dp", "ctx", None),
            P(None, ("dp", "ctx")),
            P(None, ("dp", "ctx")),
            P(None, ("dp", "ctx"), None),
            P(None, ("dp", "ctx")),
            P(None, ("dp", "ctx")),
            P(None, ("dp", "ctx"), None),
            P(None, ("dp", "ctx")),
            P(None, ("dp", "ctx")),
            P(None, ("dp", "ctx")),
            P(None, ("dp", "ctx"), None),
            P(None, ("dp", "ctx")),
            P(None, ("dp", "ctx"), None),
            P(None, ("dp", "ctx")),
        ),
        out_specs=(
            P("dp", "ctx", None),
            P("dp", "ctx", None),
            P(None, ("dp", "ctx")),
            P(None, ("dp", "ctx")),
            P(None, ("dp", "ctx"), None),
            P(None, ("dp", "ctx")),
            P(None, ("dp", "ctx")),
            P(None, ("dp", "ctx"), None),
            P(None, ("dp", "ctx")),
            P(None, ("dp", "ctx")),
            P(None, ("dp", "ctx")),
            P(None, ("dp", "ctx"), None),
            P(None, ("dp", "ctx")),
            P(None, ("dp", "ctx"), None),
            P(None, ("dp", "ctx")),
        ),
        check_vma=False,
    )
```

```python
import functools
import math

import jax
import jax.numpy as jnp
from jax import lax
from jax.experimental import pallas as pl
from jax.experimental.pallas import tpu as pltpu
from jax.sharding import PartitionSpec as P

HEAD = 64
LAYERS = 2
DOCS = 8


norm_eps = 1e-05
masked_value = -1e30
gelu_coeff = 0.7978845608028654
cubic_coeff = 0.044715

def swap(value, dp_bits, ctx_bits):
    dp_size, ctx_size = lax.axis_size("dp"), lax.axis_size("ctx")
    pairs = [
        (i, ((i // ctx_size) ^ dp_bits) * ctx_size + ((i % ctx_size) ^ ctx_bits))
        for i in range(dp_size * ctx_size)
    ]
    return lax.ppermute(value, ("dp", "ctx"), pairs)


def flip(index, bits):
    bit = 1
    while bit <= bits:
        if bits & bit:
            index = index + bit * (1 - 2 * ((index // bit) % 2))
        bit *= 2
    return index


def pick(value, place, axis):
    return lax.dynamic_index_in_dim(value, place, axis, keepdims=False)


class Route:
    def __init__(self, phases, chips):
        self.phases, self.chips = phases, chips
        self.dp, ctx = lax.axis_index("dp"), lax.axis_index("ctx")
        self.chip, self.core = ctx // 2, ctx % 2

    def over(self, s, side):
        rising, falling = self.dp, self.dp
        for p in range(self.phases):
            if s >> p & 1:
                rising, falling = flip(rising, 1 << p), flip(falling, 1 << (self.phases - 1 - p))
        return (1 - side) * rising + side * falling

    def row(self, s, k, side):
        return self.over(s, side) * self.chips + flip(self.chip, k)

    def phase_partner(self, p):
        return (self.over(1 << p, self.core), 2 * self.chip + self.core)

    def chip_partner(self, k):
        return (self.dp, 2 * flip(self.chip, k) + self.core)

    def core_partner(self):
        return (self.dp, 2 * self.chip + 1 - self.core)

    def meet(self, cores):
        partners = [self.phase_partner(p) for p in range(self.phases)]
        partners += [self.chip_partner(k) for k in range(1, self.chips)]
        if cores:
            partners.append(self.core_partner())
        barrier = pltpu.get_barrier_semaphore()
        for partner in partners:
            pl.semaphore_signal(
                barrier, inc=1, device_id=partner, device_id_type=pl.DeviceIdType.MESH
            )
        pl.semaphore_wait(barrier, len(partners))


def send(source, target, leave, arrive, device):
    copy = pltpu.make_async_remote_copy(
        src_ref=source,
        dst_ref=target,
        send_sem=leave,
        recv_sem=arrive,
        device_id=device,
        device_id_type=pl.DeviceIdType.MESH,
    )
    copy.start()
    return copy


def cut(shape, most):
    rows, columns = shape
    if rows * columns <= most:
        return [(slice(0, rows), slice(0, columns))]
    if columns > 512:
        step = max(128, most // rows // 128 * 128)
        return [
            (slice(0, rows), slice(at, min(at + step, columns))) for at in range(0, columns, step)
        ]
    step = max(16, most // columns // 16 * 16)
    return [(slice(at, min(at + step, rows)), slice(0, columns)) for at in range(0, rows, step)]


def span(part, base=0):
    start = base + part.start if isinstance(base, int) else pl.multiple_of(base + part.start, 128)
    return pl.ds(start, part.stop - part.start)


def gather_kernel(phases, chips, count, *refs):
    owns, wholes = refs[:count], refs[count : 2 * count]
    place_sem, leave, arrive, give, take = refs[2 * count :]
    route = Route(phases, chips)
    route.meet(True)
    items = [(w, *piece) for w in range(count) for piece in cut(owns[w].shape, 80000)]

    def spot(n, s, k, side):
        w, rows, columns = items[n]
        whole, row = wholes[w], route.row(s, k, side)
        if len(whole.shape) == 4:
            return whole.at[row, side]
        return whole.at[row, span(rows), span(columns, side * owns[w].shape[-1])]

    travels, gifts, placed = {}, [], []

    def forward(n, s, k):
        target = spot(n, s, k, route.core)
        w, rows, columns = items[n]
        source = owns[w].at[span(rows), span(columns)] if s == 0 and k == 0 else target
        if s == 0 and k == 0:
            for z in range(1, chips):
                travels[n, 0, z] = send(
                    source, target, leave.at[n, 0, z], arrive.at[n, 0, z], route.chip_partner(z)
                )
        for p in range(s.bit_length(), phases):
            after = s | 1 << p
            travels[n, after, k] = send(
                source, target, leave.at[n, after, k], arrive.at[n, after, k], route.phase_partner(p)
            )
        gifts.append(send(source, target, give.at[n, s, k], take.at[n, s, k], route.core_partner()))
        return source, target

    for n in range(len(items)):
        source, target = forward(n, 0, 0)
        copy = pltpu.make_async_copy(source, target, place_sem.at[n])
        copy.start()
        placed.append(copy)
    schedule = sorted(
        (n + k + s.bit_count(), n, s, k)
        for n in range(len(items))
        for s in range(1 << phases)
        for k in range(chips)
        if s or k
    )
    for _, n, s, k in schedule:
        travels[n, s, k].wait_recv()
        forward(n, s, k)
    for copy in placed:
        copy.wait()
    for copy in travels.values():
        copy.wait_send()
    for copy in gifts:
        copy.wait()


def gather_many(owns, collective_id):
    dp_size, chips = lax.axis_size("dp"), lax.axis_size("ctx") // 2
    phases, count = dp_size.bit_length() - 1, len(owns)
    total = dp_size * chips
    items = sum(len(cut(own.shape, 80000)) for own in owns)
    shapes = []
    for own in owns:
        rows, columns = own.shape
        shape = (total, 2, rows, columns) if rows == 8 else (total, rows, 2 * columns)
        shapes.append(jax.ShapeDtypeStruct(shape, own.dtype))
    slots = (items, 1 << phases, chips)
    return pl.pallas_call(
        functools.partial(gather_kernel, phases, chips, count),
        out_shape=tuple(shapes),
        in_specs=[pl.BlockSpec(memory_space=pl.ANY)] * count,
        out_specs=(pl.BlockSpec(memory_space=pl.ANY),) * count,
        scratch_shapes=[pltpu.SemaphoreType.DMA((items,))]
        + [pltpu.SemaphoreType.DMA(slots)] * 4,
        compiler_params=pltpu.CompilerParams(collective_id=collective_id, has_side_effects=True),
        cost_estimate=pl.CostEstimate(
            flops=15 * 10**9 * count, transcendentals=0, bytes_accessed=10**6 * count
        ),
    )(*owns)


def gather_far(shard):
    return lax.all_gather(shard, ("dp", "ctx"), axis=0, tiled=True)


def reduce_kernel(phases, chips, count, pieces, *refs):
    parts, outs = refs[:count], refs[count : 2 * count]
    items = len(pieces)
    refs = refs[2 * count :]
    sums, landed = refs[:items], refs[items : 2 * items]
    leave, arrive = refs[2 * items :]
    route = Route(phases, chips)
    route.meet(False)
    slots = 1 << phases

    def bit_of(s):
        return (s & -s).bit_length() - 1 if s else phases

    def order(kept):
        return [
            (s, k)
            for s in sorted(kept, key=lambda s: (bit_of(s), s))
            for k in [*range(1, chips), 0]
        ]

    def seat(p, s):
        return slots - (slots >> p) + (s >> (p + 1))

    def term(n, s, k):
        w, rows, columns = pieces[n]
        return parts[w].at[route.row(s, k, route.core), span(rows), span(columns)]

    travels, waiting = {}, []

    def flush():
        while waiting:
            n, p, s, k = waiting.pop()
            place = (seat(p, s ^ 1 << p), k) if p < phases else (slots - 1, k)
            travels[n, p, place] = send(
                term(n, s, k) if p == 0 else sums[n].at[s >> 1, k],
                landed[n].at[place],
                leave.at[(n, *place)],
                arrive.at[(n, *place)],
                route.phase_partner(p) if p < phases else route.chip_partner(k),
            )

    for n in range(items):
        for s, k in order([s for s in range(slots) if s % 2 == 0]):
            waiting.append((n, 0, s ^ 1, k))
            flush()
    for n in range(items):
        for p in range(phases):
            for s, k in order([s for s in range(slots) if bit_of(s) > p]):
                place = (seat(p, s), k)
                travels[n, p, place].wait_recv()
                if p == phases - 1 and k == 0:
                    continue
                before = term(n, s, k)[...] if p == 0 else sums[n][s >> 1, k]
                added = before.astype(jnp.float32) + landed[n][place].astype(jnp.float32)
                flush()
                sums[n][s >> 1, k] = added.astype(before.dtype)
                if bit_of(s) == p + 1 and (s or k):
                    waiting.append((n, p + 1, s, k))
            flush()
    for n, (w, rows, columns) in enumerate(pieces):
        last = (seat(phases - 1, 0), 0)
        before = term(n, 0, 0)[...] if phases == 1 else sums[n][0, 0]
        total = before.astype(jnp.float32) + landed[n][last].astype(jnp.float32)
        for k in range(1, chips):
            place = (slots - 1, k)
            travels[n, phases, place].wait_recv()
            total = total + landed[n][place].astype(jnp.float32)
        outs[w][rows, columns] = total
    for copy in travels.values():
        copy.wait_send()


def reduce_many(parts, collective_id):
    dp_size, chips = lax.axis_size("dp"), lax.axis_size("ctx") // 2
    phases, count = dp_size.bit_length() - 1, len(parts)
    slots = 1 << phases
    pieces = [(w, *piece) for w, part in enumerate(parts) for piece in cut(part.shape[1:], 36864)]
    sizes = [
        ((rows.stop - rows.start, columns.stop - columns.start), parts[w].dtype)
        for w, rows, columns in pieces
    ]
    return pl.pallas_call(
        functools.partial(reduce_kernel, phases, chips, count, pieces),
        out_shape=tuple(jax.ShapeDtypeStruct(part.shape[1:], jnp.float32) for part in parts),
        in_specs=[pl.BlockSpec(memory_space=pltpu.VMEM)] * count,
        out_specs=(pl.BlockSpec(memory_space=pltpu.VMEM),) * count,
        scratch_shapes=[pltpu.VMEM((slots // 2, chips, *size), dtype) for size, dtype in sizes]
        + [pltpu.VMEM((slots, chips, *size), dtype) for size, dtype in sizes]
        + [pltpu.SemaphoreType.DMA((len(pieces), slots, chips))] * 2,
        compiler_params=pltpu.CompilerParams(collective_id=collective_id, has_side_effects=True),
        cost_estimate=pl.CostEstimate(
            flops=15 * 10**9 * count, transcendentals=0, bytes_accessed=10**6 * count
        ),
    )(*parts)


def chip_rows(shards):
    core = lax.axis_index("ctx") % 2
    half = shards.shape[2] // 2
    kept = lax.dynamic_slice_in_dim(shards, core * half, half, 2)
    got = swap(lax.dynamic_slice_in_dim(shards, (1 - core) * half, half, 2), 0, 1)
    return jnp.where(
        core == 0, jnp.concatenate([kept, got], axis=1), jnp.concatenate([got, kept], axis=1)
    )


def chip_part(left, right, left_dim=0, right_dim=0):
    dp_size, chips = lax.axis_size("dp"), lax.axis_size("ctx") // 2
    core = lax.axis_index("ctx") % 2
    half = right.shape[1 - right_dim] // 2
    own_side = lax.dynamic_slice_in_dim(right, core * half, half, 1 - right_dim)
    far_side = lax.dynamic_slice_in_dim(right, (1 - core) * half, half, 1 - right_dim)
    got = swap(contract(left, far_side, left_dim, right_dim).astype(jnp.bfloat16), 0, 1)
    part = (contract(left, own_side, left_dim, right_dim) + got.astype(jnp.float32)).astype(
        jnp.bfloat16
    )
    return part.reshape(dp_size * chips, -1, half)


def device_rows(total):
    core = lax.axis_index("ctx") % 2
    total = total.reshape(2, -1, total.shape[1])
    got = swap(pick(total, 1 - core, 0), 0, 1)
    kept = pick(total, core, 0)
    return jnp.where(
        core == 0,
        jnp.concatenate([kept, got], axis=1),
        jnp.concatenate([got, kept], axis=1),
    )


def layer_norm(residual, norm_gain, norm_bias):
    row_mean = jnp.mean(residual, axis=-1, keepdims=True)
    centered = residual - row_mean
    variance = jnp.mean(centered * centered, axis=-1, keepdims=True)
    inv_std = lax.rsqrt(variance + norm_eps)
    normed = centered * inv_std
    return (normed * norm_gain + norm_bias, normed, inv_std)


def norm_back(grad_norm, normed, inv_std, norm_gain):
    scaled = grad_norm * norm_gain
    return inv_std * (
        scaled
        - jnp.mean(scaled, axis=-1, keepdims=True)
        - normed * jnp.mean(scaled * normed, axis=-1, keepdims=True)
    )


def gelu_value(values_in):
    inner_arg = gelu_coeff * (values_in + cubic_coeff * values_in * values_in * values_in)
    return 0.5 * values_in * (1.0 + jnp.tanh(inner_arg))


def gelu_slope(values_in):
    tanh_val = jnp.tanh(gelu_coeff * (values_in + cubic_coeff * values_in * values_in * values_in))
    return 0.5 * (1.0 + tanh_val) + 0.5 * values_in * (1.0 - tanh_val * tanh_val) * gelu_coeff * (
        1.0 + 3.0 * cubic_coeff * values_in * values_in
    )


def fetch(pairs):
    copies = [pltpu.make_async_copy(*pair) for pair in pairs]
    for copy in copies:
        copy.start()
    for copy in copies:
        copy.wait()


def contract(left, right, left_dim, right_dim):
    return lax.dot_general(
        left, right, (((left_dim,), (right_dim,)), ((), ())), preferred_element_type=jnp.float32
    )


def allowed_keys(key_chunk, starts, length, own):
    places = lax.broadcasted_iota(jnp.int32, (length, length), 0)
    allowed = places + key_chunk * length >= starts
    if own:
        allowed &= places <= lax.broadcasted_iota(jnp.int32, (length, length), 1)
    return allowed


def mix_kernel(parts, shares, *refs):
    first_ref, starts_ref = refs[:2]
    mine, theirs = refs[2 : 2 + parts], refs[2 + parts]
    out_ref, log_ref, queries, both, total, sems = refs[3 + parts :]
    width, length = out_ref.shape[1:]
    ctx_rank = lax.axis_index("ctx")
    part, share = ctx_rank // shares, ctx_rank % shares
    pairs = []
    for k in range(parts):
        chunk = (part ^ k) * shares
        pairs.append((mine[k].at[pl.ds(0, width)], queries.at[k], sems.at[k, 0]))
        pairs.append(
            (mine[k].at[pl.ds(width, 2 * width)], both.at[chunk + share], sems.at[k, 1])
        )
        for j in range(1, shares):
            pairs.append((theirs.at[j - 1, k], both.at[chunk + (share ^ j)], sems.at[k, 1 + j]))
    fetch(pairs)
    heads = width // HEAD

    def one_chunk(k, carry):
        chunk = (part ^ k) * shares + share
        starts = starts_ref[chunk]
        total[...] = jnp.zeros_like(total)

        def block(key_chunk, state, own):
            allowed = allowed_keys(key_chunk, starts, length, own)
            following = []
            for head in range(heads):
                top, weight = state[head]
                rows = slice(head * HEAD, (head + 1) * HEAD)
                value_rows = slice(width + head * HEAD, width + (head + 1) * HEAD)
                score = contract(both[key_chunk, rows], queries[k, rows], 0, 0)
                score = jnp.where(allowed, score, masked_value)
                new_top = jnp.maximum(top, jnp.max(score, axis=0, keepdims=True))
                prob = jnp.exp(score - new_top)
                shrink = jnp.exp(top - new_top)
                weight = weight * shrink + jnp.sum(prob, axis=0, keepdims=True)
                total[rows] = total[rows] * shrink + contract(
                    both[key_chunk, value_rows], prob.astype(jnp.bfloat16), 1, 0
                )
                following.append((new_top, weight))
            return tuple(following)

        empty = (
            jnp.full((1, length), masked_value, jnp.float32),
            jnp.zeros((1, length), jnp.float32),
        )
        state = lax.fori_loop(
            first_ref[chunk], chunk, lambda at, s: block(at, s, False), (empty,) * heads
        )
        state = block(chunk, state, True)
        for head in range(heads):
            top, weight = state[head]
            rows = slice(head * HEAD, (head + 1) * HEAD)
            out_ref[k, rows] = (total[rows] / weight).astype(out_ref.dtype)
            log_ref[k, head : head + 1] = top + jnp.log(weight)
        return carry

    lax.fori_loop(0, parts, one_chunk, 0)


def mix_back_kernel(parts, shares, *refs):
    first_ref, starts_ref, mixed, log_ref = refs[:4]
    mine, grads, theirs = refs[4 : 4 + parts], refs[4 + parts : 4 + 2 * parts], refs[4 + 2 * parts]
    out_ref, own_ref, far_ref, queries, both, slopes, totals, sems = refs[5 + 2 * parts :]
    width, length = out_ref.shape[1:]
    ctx_rank = lax.axis_index("ctx")
    part, share = ctx_rank // shares, ctx_rank % shares
    pairs = []
    for k in range(parts):
        chunk = (part ^ k) * shares
        pairs.append((mine[k].at[pl.ds(0, width)], queries.at[k], sems.at[k, 0]))
        pairs.append((grads[k], slopes.at[k], sems.at[k, 1]))
        pairs.append(
            (mine[k].at[pl.ds(width, 2 * width)], both.at[chunk + share], sems.at[k, 2])
        )
        for j in range(1, shares):
            pairs.append((theirs.at[j - 1, k], both.at[chunk + (share ^ j)], sems.at[k, 2 + j]))
    fetch(pairs)
    totals[...] = jnp.zeros_like(totals)
    heads = width // HEAD

    def one_chunk(k, carry):
        chunk = (part ^ k) * shares + share
        starts = starts_ref[chunk]
        deltas, logs = [], []
        for head in range(heads):
            rows = slice(head * HEAD, (head + 1) * HEAD)
            deltas.append(
                jnp.sum(
                    slopes[k, rows].astype(jnp.float32) * mixed[k, rows].astype(jnp.float32),
                    axis=0,
                    keepdims=True,
                )
            )
            logs.append(log_ref[k, head : head + 1])

        def block(key_chunk, state, own):
            allowed = allowed_keys(key_chunk, starts, length, own)
            following = []
            for head in range(heads):
                rows = slice(head * HEAD, (head + 1) * HEAD)
                value_rows = slice(width + head * HEAD, width + (head + 1) * HEAD)
                keys, values = both[key_chunk, rows], both[key_chunk, value_rows]
                asked, slope = queries[k, rows], slopes[k, rows]
                score = contract(keys, asked, 0, 0)
                prob = jnp.exp(jnp.where(allowed, score - logs[head], masked_value))
                grad_prob = contract(values, slope, 0, 0)
                grad_score = (prob * (grad_prob - deltas[head])).astype(jnp.bfloat16)
                totals[key_chunk, value_rows] += contract(slope, prob.astype(jnp.bfloat16), 1, 1)
                totals[key_chunk, rows] += contract(asked, grad_score, 1, 1)
                following.append(state[head] + contract(keys, grad_score, 1, 0))
            return tuple(following)

        zero = jnp.zeros((HEAD, length), jnp.float32)
        state = lax.fori_loop(
            first_ref[chunk], chunk, lambda at, s: block(at, s, False), (zero,) * heads
        )
        state = block(chunk, state, True)
        for head in range(heads):
            rows = slice(head * HEAD, (head + 1) * HEAD)
            out_ref[k, rows] = (state[head] * HEAD ** (-0.5)).astype(out_ref.dtype)
        return carry

    lax.fori_loop(0, parts, one_chunk, 0)
    for k in range(parts):
        chunk = (part ^ k) * shares
        own_ref[k] = totals[chunk + share]
        for j in range(1, shares):
            far_ref[j - 1, k] = totals[chunk + (share ^ j)].astype(far_ref.dtype)


def spread(grouped, parts, shares):
    part = lax.axis_index("ctx") // shares
    return [
        pick(grouped, part ^ k, 0) if k == 0 else swap(pick(grouped, part ^ k, 0), 0, shares * k)
        for k in range(parts)
    ]


def collect(pieces, parts, shares):
    part = lax.axis_index("ctx") // shares
    held = jnp.stack([p if k == 0 else swap(p, 0, shares * k) for k, p in enumerate(pieces)])
    return jnp.concatenate([pick(held, part ^ j, 0) for j in range(parts)])


def attend(mine, theirs, starts, first, parts, shares):
    width, length = mine[0].shape[0] // 3, mine[0].shape[1]
    mixed, logs = pl.pallas_call(
        functools.partial(mix_kernel, parts, shares),
        out_shape=(
            jax.ShapeDtypeStruct((parts, width, length), jnp.bfloat16),
            jax.ShapeDtypeStruct((parts, 8, length), jnp.float32),
        ),
        in_specs=[
            pl.BlockSpec(memory_space=pltpu.SMEM),
            pl.BlockSpec(memory_space=pltpu.VMEM),
        ]
        + [pl.BlockSpec(memory_space=pl.ANY)] * (parts + 1),
        out_specs=(pl.BlockSpec(memory_space=pltpu.VMEM),) * 2,
        scratch_shapes=[
            pltpu.VMEM((parts, width, length), jnp.bfloat16),
            pltpu.VMEM((parts * shares, 2 * width, length), jnp.bfloat16),
            pltpu.VMEM((width, length), jnp.float32),
            pltpu.SemaphoreType.DMA((parts, 1 + shares)),
        ],
        cost_estimate=pl.CostEstimate(
            flops=2 * parts * parts * shares * length * length * width * 2,
            transcendentals=0,
            bytes_accessed=4 * parts * width * length * 2,
        ),
    )(first, starts, *mine, theirs)
    return mixed, logs


def attend_back(grads, kept, starts, first, parts, shares):
    mixed, logs, mine, theirs = kept
    width, length = mixed.shape[1:]
    grad_queries, own, far = pl.pallas_call(
        functools.partial(mix_back_kernel, parts, shares),
        out_shape=(
            jax.ShapeDtypeStruct((parts, width, length), jnp.bfloat16),
            jax.ShapeDtypeStruct((parts, 2 * width, length), jnp.float32),
            jax.ShapeDtypeStruct((shares - 1, parts, 2 * width, length), jnp.bfloat16),
        ),
        in_specs=[
            pl.BlockSpec(memory_space=pltpu.SMEM),
            pl.BlockSpec(memory_space=pltpu.VMEM),
            pl.BlockSpec(memory_space=pltpu.VMEM),
            pl.BlockSpec(memory_space=pltpu.VMEM),
        ]
        + [pl.BlockSpec(memory_space=pl.ANY)] * (2 * parts + 1),
        out_specs=(pl.BlockSpec(memory_space=pltpu.VMEM),) * 3,
        scratch_shapes=[
            pltpu.VMEM((parts, width, length), jnp.bfloat16),
            pltpu.VMEM((parts * shares, 2 * width, length), jnp.bfloat16),
            pltpu.VMEM((parts, width, length), jnp.bfloat16),
            pltpu.VMEM((parts * shares, 2 * width, length), jnp.float32),
            pltpu.SemaphoreType.DMA((parts, 2 + shares)),
        ],
        cost_estimate=pl.CostEstimate(
            flops=5 * parts * parts * shares * length * length * width * 2,
            transcendentals=0,
            bytes_accessed=8 * parts * width * length * 2,
        ),
    )(first, starts, mixed, logs, *mine, *grads, theirs)
    return grad_queries, own, far


def forward_layer(residual, narrow, joined, held, plan, near):
    starts, first, parts, shares, qkv_scale = plan
    width = residual.shape[1]
    normed_in, normed1, inv_std1 = layer_norm(residual, narrow["gain1"], narrow["bias1"])
    attn_in = normed_in.astype(jnp.bfloat16)
    qkv_weight, out_weight = joined
    projected = (contract(qkv_weight, attn_in, 0, 1) + narrow["qkv"][:, None]) * qkv_scale[:, None]
    grouped = projected.astype(jnp.bfloat16).reshape(parts, -1, residual.shape[0])
    if not near:
        mine = spread(grouped, parts, shares)
        fc_weight, proj_weight = held
    else:
        grouped, held = lax.optimization_barrier((grouped, held))
        mine = spread(grouped, parts, shares)
        fc_weight, proj_weight = gather_many(held, 2)
    joint = jnp.stack([piece[width // parts :] for piece in mine])
    theirs = jnp.stack([swap(joint, 0, j) for j in range(1, shares)])
    if near:
        mine, theirs, fc_weight, proj_weight = lax.optimization_barrier(
            (mine, theirs, fc_weight, proj_weight)
        )
    mixed, logs = attend(mine, theirs, starts, first, parts, shares)
    kept = (mixed, logs, mine, theirs)
    mixed_columns = collect([mixed[k] for k in range(parts)], parts, shares)
    fc_weight = fc_weight.reshape(width, -1)
    proj_weight = proj_weight.reshape(-1, width)
    middle = residual + contract(mixed_columns, out_weight, 0, 0) + narrow["out"]
    normed_mid, normed2, inv_std2 = layer_norm(middle, narrow["gain2"], narrow["bias2"])
    ffn_in = normed_mid.astype(jnp.bfloat16)
    pre_act = jnp.dot(ffn_in, fc_weight, preferred_element_type=jnp.float32) + narrow["fc"]
    hidden = gelu_value(pre_act).astype(jnp.bfloat16)
    result = middle + jnp.dot(hidden, proj_weight, preferred_element_type=jnp.float32) + narrow["proj"]
    saved = (
        (normed1, inv_std1, attn_in, kept, mixed_columns, normed2, inv_std2, ffn_in, pre_act, hidden),
        (qkv_weight, out_weight, fc_weight, proj_weight),
    )
    return result, saved


def backward_layer(grad_residual, saved, narrow, plan, carried):
    (
        (normed1, inv_std1, attn_in, kept, mixed_columns, normed2, inv_std2, ffn_in, pre_act, hidden),
        (qkv_weight, out_weight, fc_weight, proj_weight),
    ) = saved
    starts, first, parts, shares, _ = plan
    grad_narrow = grad_residual.astype(jnp.bfloat16)
    grad_proj_w = chip_part(hidden, grad_narrow)
    grad_proj_b = jnp.sum(grad_residual, axis=0)
    grad_hidden = contract(grad_narrow, proj_weight, 1, 1)
    grad_pre = grad_hidden * gelu_slope(pre_act)
    pre_narrow = grad_pre.astype(jnp.bfloat16)
    grad_fc_w = chip_part(ffn_in, pre_narrow)
    grad_fc_b = jnp.sum(grad_pre, axis=0)
    grad_norm2 = contract(pre_narrow, fc_weight, 1, 1)
    grad_gain2 = jnp.sum(grad_norm2 * normed2, axis=0)
    grad_bias2 = jnp.sum(grad_norm2, axis=0)
    grad_middle = grad_residual + norm_back(grad_norm2, normed2, inv_std2, narrow["gain2"])
    middle_narrow = grad_middle.astype(jnp.bfloat16)
    grad_out_w = chip_part(mixed_columns, middle_narrow, left_dim=1)
    grad_out_b = jnp.sum(grad_middle, axis=0)
    grad_mixed = contract(out_weight, middle_narrow, 1, 1).astype(jnp.bfloat16)
    grad_mixed = grad_mixed.reshape(parts, -1, grad_mixed.shape[1])
    grads = spread(grad_mixed, parts, shares)
    grad_queries, own, far = attend_back(grads, kept, starts, first, parts, shares)
    for j in range(1, shares):
        own = own + swap(far[j - 1], 0, j).astype(jnp.float32)
    joint = jnp.concatenate([grad_queries, own.astype(jnp.bfloat16)], axis=1)
    terms = [grad_proj_w, grad_fc_w, grad_out_w, *carried]
    joint, terms = lax.optimization_barrier((joint, terms))
    grad_qkv = collect([joint[k] for k in range(parts)], parts, shares)
    sums = reduce_many(terms, 4 + len(carried))
    grad_qkv, sums = lax.optimization_barrier((grad_qkv, sums))
    grad_qkv_w = chip_part(attn_in, grad_qkv, right_dim=1)
    grad_qkv_b = jnp.sum(grad_qkv.astype(jnp.float32), axis=1).reshape(parts, 3, -1)
    grad_norm1 = contract(grad_qkv, qkv_weight, 0, 1)
    grad_gain1 = jnp.sum(grad_norm1 * normed1, axis=0)
    grad_bias1 = jnp.sum(grad_norm1, axis=0)
    grad_before = grad_middle + norm_back(grad_norm1, normed1, inv_std1, narrow["gain1"])
    vectors = (
        grad_gain1,
        grad_bias1,
        grad_qkv_b[:, 0].reshape(-1),
        grad_qkv_b[:, 2].reshape(-1),
        grad_out_b,
        grad_gain2,
        grad_bias2,
        grad_proj_b,
    )
    return grad_before, grad_qkv_w, sums, vectors, grad_fc_b


def by_part(columns, parts):
    rows = columns.shape[0]
    return jnp.swapaxes(columns.reshape(rows, 3, parts, -1), 1, 2).reshape(rows, -1)


def by_kind(columns, parts):
    rows = columns.shape[0]
    return jnp.swapaxes(columns.reshape(rows, parts, 3, -1), 1, 2).reshape(rows, -1)


def shards(
    block_input,
    doc_ids,
    out_grad,
    ln1_gain,
    ln1_bias,
    w_qkv,
    b_query,
    b_value,
    w_out,
    b_out,
    ln2_gain,
    ln2_bias,
    w_fc,
    b_fc,
    w_proj,
    b_proj,
):
    seq_count, local_len, model_width = block_input.shape
    row_count = seq_count * local_len
    dp_size, ctx_size = lax.axis_size("dp"), lax.axis_size("ctx")
    devices = dp_size * ctx_size
    parts = math.gcd(model_width // HEAD, ctx_size)
    shares = ctx_size // parts
    narrow_list = (ln1_gain, ln1_bias, b_query, b_value, b_out, ln2_gain, ln2_bias, b_proj)
    narrow_count = LAYERS * len(narrow_list)
    slot = narrow_list[0].shape[1]
    fc_slot = b_fc.shape[1]
    used = narrow_count * slot + LAYERS * fc_slot
    packed_size = -(-(used + row_count) // 1024) * 1024
    packed = jnp.concatenate(
        [
            jnp.stack(narrow_list, 1).reshape(-1),
            b_fc.reshape(-1),
            doc_ids.reshape(-1).astype(jnp.bfloat16),
            jnp.zeros((packed_size - used - row_count,), jnp.bfloat16),
        ]
    )
    joined_pieces = chip_rows(jnp.concatenate([by_part(w_qkv[0], parts), w_out[0]], axis=1)[None])[0]
    fc_pieces, proj_pieces = chip_rows(w_fc[:1])[0], chip_rows(w_proj[:1])[0]
    joined, small = gather_many([joined_pieces, packed.reshape(8, -1)], 1)
    later_shards = (w_qkv[1:], w_out[1:], w_fc[1:], w_proj[1:])
    joined = joined.reshape(model_width, -1)
    far_weights = [
        (
            (gather_far(by_part(qkv, parts)), gather_far(out)),
            (gather_far(fc), gather_far(proj)),
        )
        for qkv, out, fc, proj in zip(*later_shards)
    ]
    near_weights = (
        (joined[:, : 3 * model_width], joined[:, 3 * model_width :]),
        (fc_pieces, proj_pieces),
    )
    small = small.reshape(devices, -1)
    narrow_all = (
        jnp.transpose(
            small[:, : narrow_count * slot].reshape(devices, narrow_count, slot), (1, 0, 2)
        )
        .reshape(LAYERS, len(narrow_list), devices * slot)
        .astype(jnp.float32)
    )
    fc_all = (
        jnp.transpose(
            small[:, narrow_count * slot : used].reshape(devices, LAYERS, fc_slot), (1, 0, 2)
        )
        .reshape(LAYERS, devices * fc_slot)
        .astype(jnp.float32)
    )
    ids = pick(
        small[:, used : used + row_count].reshape(dp_size, ctx_size, row_count),
        lax.axis_index("dp"),
        0,
    )
    ids = lax.optimization_barrier(ids.astype(jnp.int32))
    starts = jnp.zeros((ctx_size, row_count), jnp.int32)
    for number in range(DOCS):
        before = jnp.sum((ids < number).astype(jnp.int32))
        starts = jnp.where(ids == number, before, starts)
    first = starts[:, 0] // row_count
    qkv_scale = jnp.tile(
        jnp.concatenate(
            [
                jnp.full((model_width // parts,), HEAD ** (-0.5), jnp.float32),
                jnp.ones((2 * model_width // parts,), jnp.float32),
            ]
        ),
        parts,
    )

    plan = (starts.reshape(ctx_size, 1, row_count), first, parts, shares, qkv_scale)

    residual = block_input.reshape(row_count, model_width).astype(jnp.float32)
    narrow_sets, saved_list = [], []
    for layer_idx in range(LAYERS):
        rows = narrow_all[layer_idx]
        narrow = dict(
            zip(("gain1", "bias1", "query", "value", "out", "gain2", "bias2", "proj"), rows)
        )
        narrow["fc"] = fc_all[layer_idx]
        narrow["qkv"] = by_part(
            jnp.concatenate([rows[2], jnp.zeros_like(rows[2]), rows[3]])[None], parts
        )[0]
        residual, saved = forward_layer(
            residual, narrow, *([near_weights] + far_weights)[layer_idx], plan, layer_idx == 0
        )
        narrow_sets.append(narrow)
        saved_list.append(saved)
    output_rows = residual.astype(jnp.bfloat16).reshape(seq_count, local_len, model_width)
    grad_residual = out_grad.reshape(row_count, model_width).astype(jnp.float32)
    qkv_sums, other_sums, vector_sets, fc_sets = ([None] * LAYERS for _ in range(4))
    carried = []
    for layer_idx in reversed(range(LAYERS)):
        grad_residual, part, sums, vector_sets[layer_idx], fc_sets[layer_idx] = backward_layer(
            grad_residual, saved_list[layer_idx], narrow_sets[layer_idx], plan, carried
        )
        other_sums[layer_idx] = sums[:3]
        if carried:
            qkv_sums[layer_idx + 1] = sums[3]
        carried = [part]
    grad_rows = grad_residual.astype(jnp.bfloat16).reshape(seq_count, local_len, model_width)
    term_size = -(-used // 1024) * 1024
    narrow_terms = jnp.stack([vector for vectors in vector_sets for vector in vectors])
    fc_terms = jnp.stack(fc_sets)
    terms = jnp.concatenate(
        [
            jnp.transpose(narrow_terms.reshape(narrow_count, devices, slot), (1, 0, 2)).reshape(
                devices, -1
            ),
            jnp.transpose(fc_terms.reshape(LAYERS, devices, fc_slot), (1, 0, 2)).reshape(
                devices, -1
            ),
            jnp.zeros((devices, term_size - used), jnp.float32),
        ],
        axis=1,
    )
    terms = terms.reshape(devices // 2, 2, 8, term_size // 8)
    core = lax.axis_index("ctx") % 2
    terms = pick(terms, core, 1) + swap(pick(terms, 1 - core, 1), 0, 1)
    qkv_sums[0], sums = reduce_many([*carried, terms], 6)
    sums = sums.reshape(-1)
    narrow_sums = sums[: narrow_count * slot].reshape(LAYERS, len(narrow_list), slot)
    grad_fc_b = sums[narrow_count * slot : used].reshape(LAYERS, fc_slot)
    grad_w_qkv = jnp.stack([by_kind(device_rows(total), parts) for total in qkv_sums])
    grad_w_proj, grad_w_fc, grad_w_out = (
        jnp.stack([device_rows(sums[n]) for sums in other_sums]) for n in range(3)
    )
    return (
        output_rows,
        grad_rows,
        narrow_sums[:, 0],
        narrow_sums[:, 1],
        grad_w_qkv,
        narrow_sums[:, 2],
        narrow_sums[:, 3],
        grad_w_out,
        narrow_sums[:, 4],
        narrow_sums[:, 5],
        narrow_sums[:, 6],
        grad_w_fc,
        grad_fc_b,
        grad_w_proj,
        narrow_sums[:, 7],
    )


def solution(mesh):
    return jax.shard_map(
        shards,
        mesh=mesh,
        in_specs=(
            P("dp", "ctx", None),
            P("dp", "ctx"),
            P("dp", "ctx", None),
            P(None, ("dp", "ctx")),
            P(None, ("dp", "ctx")),
            P(None, ("dp", "ctx"), None),
            P(None, ("dp", "ctx")),
            P(None, ("dp", "ctx")),
            P(None, ("dp", "ctx"), None),
            P(None, ("dp", "ctx")),
            P(None, ("dp", "ctx")),
            P(None, ("dp", "ctx")),
            P(None, ("dp", "ctx"), None),
            P(None, ("dp", "ctx")),
            P(None, ("dp", "ctx"), None),
            P(None, ("dp", "ctx")),
        ),
        out_specs=(
            P("dp", "ctx", None),
            P("dp", "ctx", None),
            P(None, ("dp", "ctx")),
            P(None, ("dp", "ctx")),
            P(None, ("dp", "ctx"), None),
            P(None, ("dp", "ctx")),
            P(None, ("dp", "ctx")),
            P(None, ("dp", "ctx"), None),
            P(None, ("dp", "ctx")),
            P(None, ("dp", "ctx")),
            P(None, ("dp", "ctx")),
            P(None, ("dp", "ctx"), None),
            P(None, ("dp", "ctx")),
            P(None, ("dp", "ctx"), None),
            P(None, ("dp", "ctx")),
        ),
        check_vma=False,
    )
```

```python
import functools
import math

import jax
import jax.numpy as jnp
from jax import lax
from jax.experimental import pallas as pl
from jax.experimental.pallas import tpu as pltpu
from jax.sharding import PartitionSpec as P

HEAD = 64
LAYERS = 2
DOCS = 8


norm_eps = 1e-05
masked_value = -1e30
gelu_coeff = 0.7978845608028654
cubic_coeff = 0.044715

def swap(value, dp_bits, ctx_bits):
    dp_size, ctx_size = lax.axis_size("dp"), lax.axis_size("ctx")
    pairs = [
        (i, ((i // ctx_size) ^ dp_bits) * ctx_size + ((i % ctx_size) ^ ctx_bits))
        for i in range(dp_size * ctx_size)
    ]
    return lax.ppermute(value, ("dp", "ctx"), pairs)


def flip(index, bits):
    bit = 1
    while bit <= bits:
        if bits & bit:
            index = index + bit * (1 - 2 * ((index // bit) % 2))
        bit *= 2
    return index


def pick(value, place, axis):
    return lax.dynamic_index_in_dim(value, place, axis, keepdims=False)


class Route:
    def __init__(self, phases, chips):
        self.phases, self.chips = phases, chips
        self.dp, ctx = lax.axis_index("dp"), lax.axis_index("ctx")
        self.chip, self.core = ctx // 2, ctx % 2

    def over(self, s, side):
        rising, falling = self.dp, self.dp
        for p in range(self.phases):
            if s >> p & 1:
                rising, falling = flip(rising, 1 << p), flip(falling, 1 << (self.phases - 1 - p))
        return (1 - side) * rising + side * falling

    def row(self, s, k, side):
        return self.over(s, side) * self.chips + flip(self.chip, k)

    def phase_partner(self, p):
        return (self.over(1 << p, self.core), 2 * self.chip + self.core)

    def chip_partner(self, k):
        return (self.dp, 2 * flip(self.chip, k) + self.core)

    def core_partner(self):
        return (self.dp, 2 * self.chip + 1 - self.core)

    def meet(self, cores):
        partners = [self.phase_partner(p) for p in range(self.phases)]
        partners += [self.chip_partner(k) for k in range(1, self.chips)]
        if cores:
            partners.append(self.core_partner())
        barrier = pltpu.get_barrier_semaphore()
        for partner in partners:
            pl.semaphore_signal(
                barrier, inc=1, device_id=partner, device_id_type=pl.DeviceIdType.MESH
            )
        pl.semaphore_wait(barrier, len(partners))


def send(source, target, leave, arrive, device):
    copy = pltpu.make_async_remote_copy(
        src_ref=source,
        dst_ref=target,
        send_sem=leave,
        recv_sem=arrive,
        device_id=device,
        device_id_type=pl.DeviceIdType.MESH,
    )
    copy.start()
    return copy


def cut(shape, most):
    rows, columns = shape
    if rows * columns <= most:
        return [(slice(0, rows), slice(0, columns))]
    if columns > 512:
        step = max(128, most // rows // 128 * 128)
        return [
            (slice(0, rows), slice(at, min(at + step, columns))) for at in range(0, columns, step)
        ]
    step = rows // 2
    return [(slice(at, at + step), slice(0, columns)) for at in (0, step)]


def span(part, base=0):
    start = base + part.start if isinstance(base, int) else pl.multiple_of(base + part.start, 128)
    return pl.ds(start, part.stop - part.start)


def gather_kernel(phases, chips, count, *refs):
    owns, wholes = refs[:count], refs[count : 2 * count]
    place_sem, leave, arrive, give, take = refs[2 * count :]
    route = Route(phases, chips)
    route.meet(True)
    items = [(w, *piece) for w in range(count) for piece in cut(owns[w].shape, 80000)]

    def spot(n, s, k, side):
        w, rows, columns = items[n]
        whole, row = wholes[w], route.row(s, k, side)
        if len(whole.shape) == 4:
            return whole.at[row, side]
        return whole.at[row, span(rows), span(columns, side * owns[w].shape[-1])]

    travels, gifts, placed = {}, [], []

    def forward(n, s, k):
        target = spot(n, s, k, route.core)
        w, rows, columns = items[n]
        source = owns[w].at[span(rows), span(columns)] if s == 0 and k == 0 else target
        if s == 0 and k == 0:
            for z in range(1, chips):
                travels[n, 0, z] = send(
                    source, target, leave.at[n, 0, z], arrive.at[n, 0, z], route.chip_partner(z)
                )
        for p in range(s.bit_length(), phases):
            after = s | 1 << p
            travels[n, after, k] = send(
                source, target, leave.at[n, after, k], arrive.at[n, after, k], route.phase_partner(p)
            )
        gifts.append(send(source, target, give.at[n, s, k], take.at[n, s, k], route.core_partner()))
        return source, target

    for n in range(len(items)):
        source, target = forward(n, 0, 0)
        copy = pltpu.make_async_copy(source, target, place_sem.at[n])
        copy.start()
        placed.append(copy)
    schedule = sorted(
        (n + k + s.bit_count(), n, s, k)
        for n in range(len(items))
        for s in range(1 << phases)
        for k in range(chips)
        if s or k
    )
    for _, n, s, k in schedule:
        travels[n, s, k].wait_recv()
        forward(n, s, k)
    for copy in placed:
        copy.wait()
    for copy in travels.values():
        copy.wait_send()
    for copy in gifts:
        copy.wait()


def gather_many(owns, collective_id):
    dp_size, chips = lax.axis_size("dp"), lax.axis_size("ctx") // 2
    phases, count = dp_size.bit_length() - 1, len(owns)
    total = dp_size * chips
    items = sum(len(cut(own.shape, 80000)) for own in owns)
    shapes = []
    for own in owns:
        rows, columns = own.shape
        shape = (total, 2, rows, columns) if rows == 8 else (total, rows, 2 * columns)
        shapes.append(jax.ShapeDtypeStruct(shape, own.dtype))
    slots = (items, 1 << phases, chips)
    return pl.pallas_call(
        functools.partial(gather_kernel, phases, chips, count),
        out_shape=tuple(shapes),
        in_specs=[pl.BlockSpec(memory_space=pl.ANY)] * count,
        out_specs=(pl.BlockSpec(memory_space=pl.ANY),) * count,
        scratch_shapes=[pltpu.SemaphoreType.DMA((items,))]
        + [pltpu.SemaphoreType.DMA(slots)] * 4,
        compiler_params=pltpu.CompilerParams(collective_id=collective_id, has_side_effects=True),
        cost_estimate=pl.CostEstimate(
            flops=15 * 10**9 * count, transcendentals=0, bytes_accessed=10**6 * count
        ),
    )(*owns)


def gather_far(shard):
    return lax.all_gather(shard, ("dp", "ctx"), axis=0, tiled=True)


def reduce_kernel(phases, chips, count, pieces, *refs):
    parts, outs = refs[:count], refs[count : 2 * count]
    items = len(pieces)
    refs = refs[2 * count :]
    joint, sums, landed = refs[:items], refs[items : 2 * items], refs[2 * items : 3 * items]
    done = refs[3 * items : 3 * items + count]
    give, take, leave, arrive, back_leave, back_arrive, place_sem = refs[3 * items + count :]
    route = Route(phases, chips)
    route.meet(True)
    core = route.core
    slots = 1 << phases

    def bit_of(s):
        return (s & -s).bit_length() - 1 if s else phases

    def order(kept):
        return [
            (s, k)
            for s in sorted(kept, key=lambda s: (bit_of(s), s))
            for k in [*range(1, chips), 0]
        ]

    def seat(p, s):
        return slots - (slots >> p) + (s >> (p + 1))

    def mine(n, side, row):
        w, rows, columns = pieces[n]
        if len(parts[w].shape) == 4:
            return parts[w].at[row, side]
        return parts[w].at[row, span(rows), span(columns, side * (parts[w].shape[-1] // 2))]

    def chip_sum(n, s, k):
        row = route.row(s, k, core)
        return mine(n, core, row)[...].astype(jnp.float32) + joint[n][row].astype(jnp.float32)

    travels, waiting = {}, []

    def flush():
        while waiting:
            n, p, s, k = waiting.pop()
            place = (seat(p, s ^ 1 << p), k) if p < phases else (slots - 1, k)
            travels[n, p, place] = send(
                joint[n].at[route.row(s, k, core)] if p == 0 else sums[n].at[s >> 1, k],
                landed[n].at[place],
                leave.at[(n, *place)],
                arrive.at[(n, *place)],
                route.phase_partner(p) if p < phases else route.chip_partner(k),
            )

    gifts = [
        send(
            mine(n, 1 - core, slice(None)), joint[n], give.at[n], take.at[n], route.core_partner()
        )
        for n in range(items)
    ]
    for n in range(items):
        gifts[n].wait_recv()
        for s, k in order([s for s in range(slots) if s % 2 == 0]):
            added = chip_sum(n, s ^ 1, k)
            flush()
            joint[n][route.row(s ^ 1, k, core)] = added.astype(joint[n].dtype)
            waiting.append((n, 0, s ^ 1, k))
    flush()
    for n in range(items):
        for p in range(phases):
            for s, k in order([s for s in range(slots) if bit_of(s) > p]):
                place = (seat(p, s), k)
                travels[n, p, place].wait_recv()
                if p == phases - 1 and k == 0:
                    continue
                before = chip_sum(n, s, k) if p == 0 else sums[n][s >> 1, k].astype(jnp.float32)
                added = before + landed[n][place].astype(jnp.float32)
                flush()
                sums[n][s >> 1, k] = added.astype(sums[n].dtype)
                if bit_of(s) == p + 1 and (s or k):
                    waiting.append((n, p + 1, s, k))
            flush()
    trades, placed = [], []
    for n, (w, rows, columns) in enumerate(pieces):
        last = (seat(phases - 1, 0), 0)
        before = chip_sum(n, 0, 0) if phases == 1 else sums[n][0, 0].astype(jnp.float32)
        total = before + landed[n][last].astype(jnp.float32)
        for k in range(1, chips):
            place = (slots - 1, k)
            travels[n, phases, place].wait_recv()
            total = total + landed[n][place].astype(jnp.float32)
        if len(parts[w].shape) == 4:
            outs[w][...] = total
            continue
        own = outs[w].shape[0]
        for side in range(2):
            first, final = max(rows.start, side * own), min(rows.stop, (side + 1) * own)
            if first < final:
                done[w][side, first - side * own : final - side * own, columns] = total[
                    first - rows.start : final - rows.start
                ]
    for w in range(count):
        if len(parts[w].shape) == 4:
            continue
        half = done[w].shape[2]
        target = outs[w].at[:, span(slice(0, half), core * half)]
        trades.append(
            send(
                done[w].at[1 - core], target, back_leave.at[w], back_arrive.at[w], route.core_partner()
            )
        )
        copy = pltpu.make_async_copy(done[w].at[core], target, place_sem.at[w])
        copy.start()
        placed.append(copy)
    for copy in placed:
        copy.wait()
    for copy in trades:
        copy.wait()
    for copy in gifts:
        copy.wait_send()
    for copy in travels.values():
        copy.wait_send()


def reduce_many(parts, collective_id):
    dp_size, chips = lax.axis_size("dp"), lax.axis_size("ctx") // 2
    phases, count = dp_size.bit_length() - 1, len(parts)
    slots = 1 << phases
    pieces, outs, held = [], [], []
    for w, part in enumerate(parts):
        if part.ndim == 4:
            shape, out = part.shape[2:], part.shape[2:]
            held.append((1, 8, 128))
        else:
            shape, out = (part.shape[1], part.shape[2] // 2), (part.shape[1] // 2, part.shape[2])
            held.append((2, out[0], shape[1]))
        pieces += [(w, *piece) for piece in cut(shape, 36864)]
        outs.append(jax.ShapeDtypeStruct(out, jnp.float32))
    sizes = [
        ((rows.stop - rows.start, columns.stop - columns.start), parts[w].dtype)
        for w, rows, columns in pieces
    ]
    return pl.pallas_call(
        functools.partial(reduce_kernel, phases, chips, count, pieces),
        out_shape=tuple(outs),
        in_specs=[pl.BlockSpec(memory_space=pltpu.VMEM)] * count,
        out_specs=(pl.BlockSpec(memory_space=pltpu.VMEM),) * count,
        scratch_shapes=[pltpu.VMEM((slots * chips, *size), dtype) for size, dtype in sizes]
        + [pltpu.VMEM((slots // 2, chips, *size), dtype) for size, dtype in sizes]
        + [pltpu.VMEM((slots, chips, *size), dtype) for size, dtype in sizes]
        + [pltpu.VMEM(shape, jnp.float32) for shape in held]
        + [pltpu.SemaphoreType.DMA((len(pieces),))] * 2
        + [pltpu.SemaphoreType.DMA((len(pieces), slots, chips))] * 2
        + [pltpu.SemaphoreType.DMA((count,))] * 3,
        compiler_params=pltpu.CompilerParams(collective_id=collective_id, has_side_effects=True),
        cost_estimate=pl.CostEstimate(
            flops=15 * 10**9 * count, transcendentals=0, bytes_accessed=10**6 * count
        ),
    )(*parts)


def chip_rows(shards):
    core = lax.axis_index("ctx") % 2
    half = shards.shape[2] // 2
    kept = lax.dynamic_slice_in_dim(shards, core * half, half, 2)
    got = swap(lax.dynamic_slice_in_dim(shards, (1 - core) * half, half, 2), 0, 1)
    return jnp.where(
        core == 0, jnp.concatenate([kept, got], axis=1), jnp.concatenate([got, kept], axis=1)
    )


def weight_term(left, right, left_dim=0, right_dim=0):
    chips_in_all = lax.axis_size("dp") * lax.axis_size("ctx") // 2
    term = contract(left, right, left_dim, right_dim).astype(jnp.bfloat16)
    return term.reshape(chips_in_all, -1, term.shape[1])


def layer_norm(residual, norm_gain, norm_bias):
    row_mean = jnp.mean(residual, axis=-1, keepdims=True)
    centered = residual - row_mean
    variance = jnp.mean(centered * centered, axis=-1, keepdims=True)
    inv_std = lax.rsqrt(variance + norm_eps)
    normed = centered * inv_std
    return (normed * norm_gain + norm_bias, normed, inv_std)


def norm_back(grad_norm, normed, inv_std, norm_gain):
    scaled = grad_norm * norm_gain
    return inv_std * (
        scaled
        - jnp.mean(scaled, axis=-1, keepdims=True)
        - normed * jnp.mean(scaled * normed, axis=-1, keepdims=True)
    )


def gelu_value(values_in):
    inner_arg = gelu_coeff * (values_in + cubic_coeff * values_in * values_in * values_in)
    return 0.5 * values_in * (1.0 + jnp.tanh(inner_arg))


def gelu_slope(values_in):
    tanh_val = jnp.tanh(gelu_coeff * (values_in + cubic_coeff * values_in * values_in * values_in))
    return 0.5 * (1.0 + tanh_val) + 0.5 * values_in * (1.0 - tanh_val * tanh_val) * gelu_coeff * (
        1.0 + 3.0 * cubic_coeff * values_in * values_in
    )


def fetch(pairs):
    copies = [pltpu.make_async_copy(*pair) for pair in pairs]
    for copy in copies:
        copy.start()
    for copy in copies:
        copy.wait()


def contract(left, right, left_dim, right_dim):
    return lax.dot_general(
        left, right, (((left_dim,), (right_dim,)), ((), ())), preferred_element_type=jnp.float32
    )


def starts_kernel(ids_ref, starts_ref):
    ids = ids_ref[...]
    starts = jnp.zeros_like(ids)
    for number in range(1, DOCS):
        before = jnp.sum(jnp.where(ids < number, 1.0, 0.0), axis=(0, 1), keepdims=True)
        starts = jnp.where(ids == number, before, starts)
    starts_ref[...] = starts.astype(jnp.int32)


def allowed_keys(key_chunk, starts, length, own):
    places = lax.broadcasted_iota(jnp.int32, (length, length), 0)
    allowed = places + key_chunk * length >= starts
    if own:
        allowed &= places <= lax.broadcasted_iota(jnp.int32, (length, length), 1)
    return allowed


def mix_kernel(parts, shares, *refs):
    first_ref, starts_ref = refs[:2]
    mine, theirs = refs[2 : 2 + parts], refs[2 + parts]
    out_ref, log_ref, queries, both, total, sems = refs[3 + parts :]
    width, length = out_ref.shape[1:]
    ctx_rank = lax.axis_index("ctx")
    part, share = ctx_rank // shares, ctx_rank % shares
    pairs = []
    for k in range(parts):
        chunk = (part ^ k) * shares
        pairs.append((mine[k].at[pl.ds(0, width)], queries.at[k], sems.at[k, 0]))
        pairs.append(
            (mine[k].at[pl.ds(width, 2 * width)], both.at[chunk + share], sems.at[k, 1])
        )
        for j in range(1, shares):
            pairs.append((theirs.at[j - 1, k], both.at[chunk + (share ^ j)], sems.at[k, 1 + j]))
    fetch(pairs)
    heads = width // HEAD

    def one_chunk(k, carry):
        chunk = (part ^ k) * shares + share
        starts = starts_ref[chunk]
        total[...] = jnp.zeros_like(total)

        def block(key_chunk, state, own):
            allowed = allowed_keys(key_chunk, starts, length, own)
            following = []
            for head in range(heads):
                top, weight = state[head]
                rows = slice(head * HEAD, (head + 1) * HEAD)
                value_rows = slice(width + head * HEAD, width + (head + 1) * HEAD)
                score = contract(both[key_chunk, rows], queries[k, rows], 0, 0)
                score = jnp.where(allowed, score, masked_value)
                new_top = jnp.maximum(top, jnp.max(score, axis=0, keepdims=True))
                prob = jnp.exp(score - new_top)
                shrink = jnp.exp(top - new_top)
                weight = weight * shrink + jnp.sum(prob, axis=0, keepdims=True)
                total[rows] = total[rows] * shrink + contract(
                    both[key_chunk, value_rows], prob.astype(jnp.bfloat16), 1, 0
                )
                following.append((new_top, weight))
            return tuple(following)

        empty = (
            jnp.full((1, length), masked_value, jnp.float32),
            jnp.zeros((1, length), jnp.float32),
        )
        state = lax.fori_loop(
            first_ref[chunk], chunk, lambda at, s: block(at, s, False), (empty,) * heads
        )
        state = block(chunk, state, True)
        for head in range(heads):
            top, weight = state[head]
            rows = slice(head * HEAD, (head + 1) * HEAD)
            out_ref[k, rows] = (total[rows] / weight).astype(out_ref.dtype)
            log_ref[k, head : head + 1] = top + jnp.log(weight)
        return carry

    lax.fori_loop(0, parts, one_chunk, 0)


def mix_back_kernel(parts, shares, *refs):
    first_ref, starts_ref, mixed, log_ref = refs[:4]
    mine, grads, theirs = refs[4 : 4 + parts], refs[4 + parts : 4 + 2 * parts], refs[4 + 2 * parts]
    out_ref, own_ref, far_ref, queries, both, slopes, totals, sems = refs[5 + 2 * parts :]
    width, length = out_ref.shape[1:]
    ctx_rank = lax.axis_index("ctx")
    part, share = ctx_rank // shares, ctx_rank % shares
    pairs = []
    for k in range(parts):
        chunk = (part ^ k) * shares
        pairs.append((mine[k].at[pl.ds(0, width)], queries.at[k], sems.at[k, 0]))
        pairs.append((grads[k], slopes.at[k], sems.at[k, 1]))
        pairs.append(
            (mine[k].at[pl.ds(width, 2 * width)], both.at[chunk + share], sems.at[k, 2])
        )
        for j in range(1, shares):
            pairs.append((theirs.at[j - 1, k], both.at[chunk + (share ^ j)], sems.at[k, 2 + j]))
    fetch(pairs)
    totals[...] = jnp.zeros_like(totals)
    heads = width // HEAD

    def one_chunk(k, carry):
        chunk = (part ^ k) * shares + share
        starts = starts_ref[chunk]
        deltas, logs = [], []
        for head in range(heads):
            rows = slice(head * HEAD, (head + 1) * HEAD)
            deltas.append(
                jnp.sum(
                    slopes[k, rows].astype(jnp.float32) * mixed[k, rows].astype(jnp.float32),
                    axis=0,
                    keepdims=True,
                )
            )
            logs.append(log_ref[k, head : head + 1])

        def block(key_chunk, state, own):
            allowed = allowed_keys(key_chunk, starts, length, own)
            following = []
            for head in range(heads):
                rows = slice(head * HEAD, (head + 1) * HEAD)
                value_rows = slice(width + head * HEAD, width + (head + 1) * HEAD)
                keys, values = both[key_chunk, rows], both[key_chunk, value_rows]
                asked, slope = queries[k, rows], slopes[k, rows]
                score = contract(keys, asked, 0, 0)
                prob = jnp.exp(jnp.where(allowed, score - logs[head], masked_value))
                grad_prob = contract(values, slope, 0, 0)
                grad_score = (prob * (grad_prob - deltas[head])).astype(jnp.bfloat16)
                totals[key_chunk, value_rows] += contract(slope, prob.astype(jnp.bfloat16), 1, 1)
                totals[key_chunk, rows] += contract(asked, grad_score, 1, 1)
                following.append(state[head] + contract(keys, grad_score, 1, 0))
            return tuple(following)

        zero = jnp.zeros((HEAD, length), jnp.float32)
        state = lax.fori_loop(
            first_ref[chunk], chunk, lambda at, s: block(at, s, False), (zero,) * heads
        )
        state = block(chunk, state, True)
        for head in range(heads):
            rows = slice(head * HEAD, (head + 1) * HEAD)
            out_ref[k, rows] = (state[head] * HEAD ** (-0.5)).astype(out_ref.dtype)
        return carry

    lax.fori_loop(0, parts, one_chunk, 0)
    for k in range(parts):
        chunk = (part ^ k) * shares
        own_ref[k] = totals[chunk + share]
        for j in range(1, shares):
            far_ref[j - 1, k] = totals[chunk + (share ^ j)].astype(far_ref.dtype)


def spread(grouped, parts, shares, axis=0):
    part = lax.axis_index("ctx") // shares
    return [
        pick(grouped, part ^ k, axis)
        if k == 0
        else swap(pick(grouped, part ^ k, axis), 0, shares * k)
        for k in range(parts)
    ]


def collect(pieces, parts, shares):
    part = lax.axis_index("ctx") // shares
    held = jnp.stack([p if k == 0 else swap(p, 0, shares * k) for k, p in enumerate(pieces)])
    return [pick(held, part ^ j, 0) for j in range(parts)]


def attend(mine, theirs, starts, first, parts, shares):
    width, length = mine[0].shape[0] // 3, mine[0].shape[1]
    mixed, logs = pl.pallas_call(
        functools.partial(mix_kernel, parts, shares),
        out_shape=(
            jax.ShapeDtypeStruct((parts, width, length), jnp.bfloat16),
            jax.ShapeDtypeStruct((parts, 8, length), jnp.float32),
        ),
        in_specs=[
            pl.BlockSpec(memory_space=pltpu.SMEM),
            pl.BlockSpec(memory_space=pltpu.VMEM),
        ]
        + [pl.BlockSpec(memory_space=pl.ANY)] * (parts + 1),
        out_specs=(pl.BlockSpec(memory_space=pltpu.VMEM),) * 2,
        scratch_shapes=[
            pltpu.VMEM((parts, width, length), jnp.bfloat16),
            pltpu.VMEM((parts * shares, 2 * width, length), jnp.bfloat16),
            pltpu.VMEM((width, length), jnp.float32),
            pltpu.SemaphoreType.DMA((parts, 1 + shares)),
        ],
        cost_estimate=pl.CostEstimate(
            flops=2 * parts * parts * shares * length * length * width * 2,
            transcendentals=0,
            bytes_accessed=4 * parts * width * length * 2,
        ),
    )(first, starts, *mine, theirs)
    return mixed, logs


def attend_back(grads, kept, starts, first, parts, shares):
    mixed, logs, mine, theirs = kept
    width, length = mixed.shape[1:]
    grad_queries, own, far = pl.pallas_call(
        functools.partial(mix_back_kernel, parts, shares),
        out_shape=(
            jax.ShapeDtypeStruct((parts, width, length), jnp.bfloat16),
            jax.ShapeDtypeStruct((parts, 2 * width, length), jnp.float32),
            jax.ShapeDtypeStruct((shares - 1, parts, 2 * width, length), jnp.bfloat16),
        ),
        in_specs=[
            pl.BlockSpec(memory_space=pltpu.SMEM),
            pl.BlockSpec(memory_space=pltpu.VMEM),
            pl.BlockSpec(memory_space=pltpu.VMEM),
            pl.BlockSpec(memory_space=pltpu.VMEM),
        ]
        + [pl.BlockSpec(memory_space=pl.ANY)] * (2 * parts + 1),
        out_specs=(pl.BlockSpec(memory_space=pltpu.VMEM),) * 3,
        scratch_shapes=[
            pltpu.VMEM((parts, width, length), jnp.bfloat16),
            pltpu.VMEM((parts * shares, 2 * width, length), jnp.bfloat16),
            pltpu.VMEM((parts, width, length), jnp.bfloat16),
            pltpu.VMEM((parts * shares, 2 * width, length), jnp.float32),
            pltpu.SemaphoreType.DMA((parts, 2 + shares)),
        ],
        cost_estimate=pl.CostEstimate(
            flops=5 * parts * parts * shares * length * length * width * 2,
            transcendentals=0,
            bytes_accessed=8 * parts * width * length * 2,
        ),
    )(first, starts, mixed, logs, *mine, *grads, theirs)
    return grad_queries, own, far


def forward_layer(residual, narrow, joined, held, plan, collective_id):
    starts, first, parts, shares, qkv_scale = plan
    width = residual.shape[1]
    normed_in, normed1, inv_std1 = layer_norm(residual, narrow["gain1"], narrow["bias1"])
    attn_in = normed_in.astype(jnp.bfloat16)
    qkv_weight, out_weight = joined
    projected = (contract(qkv_weight, attn_in, 0, 1) + narrow["qkv"][:, None]) * qkv_scale[:, None]
    grouped = projected.astype(jnp.bfloat16).reshape(3, parts, -1, residual.shape[0])
    own, here = held
    grouped, here = lax.optimization_barrier((grouped, here))
    mine = [
        piece.reshape(-1, residual.shape[0]) for piece in spread(grouped, parts, shares, axis=1)
    ]
    gathered = gather_many(here, collective_id)
    mine, gathered = lax.optimization_barrier((mine, gathered))
    joint = jnp.stack([piece[width // parts :] for piece in mine])
    theirs = jnp.stack([swap(joint, 0, j) for j in range(1, shares)])
    fc_weight, proj_weight = (*gathered, *own)
    mixed, logs = attend(mine, theirs, starts, first, parts, shares)
    kept = (mixed, logs, mine, theirs)
    mixed_columns = jnp.concatenate(collect([mixed[k] for k in range(parts)], parts, shares))
    fc_weight = fc_weight.reshape(width, -1)
    proj_weight = proj_weight.reshape(-1, width)
    middle = residual + contract(mixed_columns, out_weight, 0, 0) + narrow["out"]
    normed_mid, normed2, inv_std2 = layer_norm(middle, narrow["gain2"], narrow["bias2"])
    ffn_in = normed_mid.astype(jnp.bfloat16)
    pre_act = jnp.dot(ffn_in, fc_weight, preferred_element_type=jnp.float32) + narrow["fc"]
    hidden = gelu_value(pre_act).astype(jnp.bfloat16)
    result = middle + jnp.dot(hidden, proj_weight, preferred_element_type=jnp.float32) + narrow["proj"]
    saved = (
        (normed1, inv_std1, attn_in, kept, mixed_columns, normed2, inv_std2, ffn_in, pre_act, hidden),
        (qkv_weight, out_weight, fc_weight, proj_weight),
    )
    return result, saved


def backward_layer(grad_residual, saved, narrow, plan, carried):
    (
        (normed1, inv_std1, attn_in, kept, mixed_columns, normed2, inv_std2, ffn_in, pre_act, hidden),
        (qkv_weight, out_weight, fc_weight, proj_weight),
    ) = saved
    starts, first, parts, shares, _ = plan
    grad_narrow = grad_residual.astype(jnp.bfloat16)
    grad_proj_w = weight_term(hidden, grad_narrow)
    grad_proj_b = jnp.sum(grad_residual, axis=0)
    grad_hidden = contract(grad_narrow, proj_weight, 1, 1)
    grad_pre = grad_hidden * gelu_slope(pre_act)
    pre_narrow = grad_pre.astype(jnp.bfloat16)
    grad_fc_w = weight_term(ffn_in, pre_narrow)
    grad_fc_b = jnp.sum(grad_pre, axis=0)
    grad_norm2 = contract(pre_narrow, fc_weight, 1, 1)
    grad_gain2 = jnp.sum(grad_norm2 * normed2, axis=0)
    grad_bias2 = jnp.sum(grad_norm2, axis=0)
    grad_middle = grad_residual + norm_back(grad_norm2, normed2, inv_std2, narrow["gain2"])
    middle_narrow = grad_middle.astype(jnp.bfloat16)
    grad_out_w = weight_term(mixed_columns, middle_narrow, left_dim=1)
    grad_out_b = jnp.sum(grad_middle, axis=0)
    grad_mixed = contract(out_weight, middle_narrow, 1, 1).astype(jnp.bfloat16)
    grad_mixed = grad_mixed.reshape(parts, -1, grad_mixed.shape[1])
    grads = spread(grad_mixed, parts, shares)
    grad_queries, own, far = attend_back(grads, kept, starts, first, parts, shares)
    for j in range(1, shares):
        own = own + swap(far[j - 1], 0, j).astype(jnp.float32)
    joint = jnp.concatenate([grad_queries, own.astype(jnp.bfloat16)], axis=1)
    terms = [grad_proj_w, grad_fc_w, grad_out_w, *carried]
    joint, terms = lax.optimization_barrier((joint, terms))
    length = joint.shape[2]
    pieces = collect([joint[k] for k in range(parts)], parts, shares)
    grad_qkv = jnp.stack([piece.reshape(3, -1, length) for piece in pieces], axis=1)
    grad_qkv = grad_qkv.reshape(-1, length)
    sums = reduce_many(terms, 4 + len(carried))
    grad_qkv, sums = lax.optimization_barrier((grad_qkv, sums))
    grad_qkv_w = weight_term(attn_in, grad_qkv, right_dim=1)
    grad_qkv_b = jnp.sum(grad_qkv.astype(jnp.float32), axis=1).reshape(3, -1)
    grad_norm1 = contract(grad_qkv, qkv_weight, 0, 1)
    grad_gain1 = jnp.sum(grad_norm1 * normed1, axis=0)
    grad_bias1 = jnp.sum(grad_norm1, axis=0)
    grad_before = grad_middle + norm_back(grad_norm1, normed1, inv_std1, narrow["gain1"])
    vectors = (
        grad_gain1,
        grad_bias1,
        grad_qkv_b[0],
        grad_qkv_b[2],
        grad_out_b,
        grad_gain2,
        grad_bias2,
        grad_proj_b,
    )
    return grad_before, grad_qkv_w, sums, vectors, grad_fc_b


def shards(
    block_input,
    doc_ids,
    out_grad,
    ln1_gain,
    ln1_bias,
    w_qkv,
    b_query,
    b_value,
    w_out,
    b_out,
    ln2_gain,
    ln2_bias,
    w_fc,
    b_fc,
    w_proj,
    b_proj,
):
    seq_count, local_len, model_width = block_input.shape
    row_count = seq_count * local_len
    dp_size, ctx_size = lax.axis_size("dp"), lax.axis_size("ctx")
    devices = dp_size * ctx_size
    parts = math.gcd(model_width // HEAD, ctx_size)
    shares = ctx_size // parts
    narrow_list = (ln1_gain, ln1_bias, b_query, b_value, b_out, ln2_gain, ln2_bias, b_proj)
    narrow_count = LAYERS * len(narrow_list)
    slot = narrow_list[0].shape[1]
    fc_slot = b_fc.shape[1]
    used = narrow_count * slot + LAYERS * fc_slot
    packed_size = -(-(used + row_count) // 1024) * 1024
    packed = jnp.concatenate(
        [
            jnp.stack(narrow_list, 1).reshape(-1),
            b_fc.reshape(-1),
            doc_ids.reshape(-1).astype(jnp.bfloat16),
            jnp.zeros((packed_size - used - row_count,), jnp.bfloat16),
        ]
    )
    joined_pieces = chip_rows(jnp.concatenate([w_qkv[:1], w_out[:1]], axis=2))[0]
    fc_pieces, proj_pieces = chip_rows(w_fc), chip_rows(w_proj[:1])[0]
    joined, small = gather_many([joined_pieces, packed.reshape(8, -1)], 1)
    joined = joined.reshape(model_width, -1)
    weights = [
        (
            (joined[:, : 3 * model_width], joined[:, 3 * model_width :]),
            ([], [fc_pieces[0], proj_pieces]),
        )
    ] + [
        (
            (gather_far(w_qkv[n]), gather_far(w_out[n])),
            ([gather_far(w_proj[n])], [fc_pieces[n]]),
        )
        for n in range(1, LAYERS)
    ]
    small = small.reshape(devices, -1)
    narrow_all = (
        jnp.transpose(
            small[:, : narrow_count * slot].reshape(devices, narrow_count, slot), (1, 0, 2)
        )
        .reshape(LAYERS, len(narrow_list), devices * slot)
        .astype(jnp.float32)
    )
    fc_all = (
        jnp.transpose(
            small[:, narrow_count * slot : used].reshape(devices, LAYERS, fc_slot), (1, 0, 2)
        )
        .reshape(LAYERS, devices * fc_slot)
        .astype(jnp.float32)
    )
    ids = pick(
        small[:, used : used + row_count].reshape(dp_size, ctx_size, row_count),
        lax.axis_index("dp"),
        0,
    )
    starts = pl.pallas_call(
        starts_kernel, out_shape=jax.ShapeDtypeStruct((ctx_size, row_count), jnp.int32)
    )(ids.astype(jnp.float32))
    first = starts[:, 0] // row_count
    qkv_scale = jnp.concatenate(
        [
            jnp.full((model_width,), HEAD ** (-0.5), jnp.float32),
            jnp.ones((2 * model_width,), jnp.float32),
        ]
    )
    plan = (starts.reshape(ctx_size, 1, row_count), first, parts, shares, qkv_scale)

    residual = block_input.reshape(row_count, model_width).astype(jnp.float32)
    narrow_sets, saved_list = [], []
    for layer_idx in range(LAYERS):
        rows = narrow_all[layer_idx]
        narrow = dict(
            zip(("gain1", "bias1", "query", "value", "out", "gain2", "bias2", "proj"), rows)
        )
        narrow["fc"] = fc_all[layer_idx]
        narrow["qkv"] = jnp.concatenate([rows[2], jnp.zeros_like(rows[2]), rows[3]])
        residual, saved = forward_layer(
            residual, narrow, *weights[layer_idx], plan, 2 if layer_idx == 0 else 3
        )
        narrow_sets.append(narrow)
        saved_list.append(saved)
    output_rows = residual.astype(jnp.bfloat16).reshape(seq_count, local_len, model_width)
    grad_residual = out_grad.reshape(row_count, model_width).astype(jnp.float32)
    qkv_sums, other_sums, vector_sets, fc_sets = ([None] * LAYERS for _ in range(4))
    carried = []
    for layer_idx in reversed(range(LAYERS)):
        grad_residual, part, sums, vector_sets[layer_idx], fc_sets[layer_idx] = backward_layer(
            grad_residual, saved_list[layer_idx], narrow_sets[layer_idx], plan, carried
        )
        other_sums[layer_idx] = sums[:3]
        if carried:
            qkv_sums[layer_idx + 1] = sums[3]
        carried = [part]
    grad_rows = grad_residual.astype(jnp.bfloat16).reshape(seq_count, local_len, model_width)
    term_size = -(-used // 1024) * 1024
    narrow_terms = jnp.concatenate([vector[None] for vectors in vector_sets for vector in vectors])
    fc_terms = jnp.concatenate([vector[None] for vector in fc_sets])
    narrow_terms, fc_terms = lax.optimization_barrier((narrow_terms, fc_terms))
    terms = jnp.concatenate(
        [
            jnp.transpose(narrow_terms.reshape(narrow_count, devices, slot), (1, 0, 2)).reshape(
                devices, -1
            ),
            jnp.transpose(fc_terms.reshape(LAYERS, devices, fc_slot), (1, 0, 2)).reshape(
                devices, -1
            ),
            jnp.zeros((devices, term_size - used), jnp.float32),
        ],
        axis=1,
    )
    terms = terms.reshape(devices // 2, 2, 8, term_size // 8)
    qkv_sums[0], sums = reduce_many([*carried, terms], 6)
    sums = sums.reshape(-1)
    narrow_sums = sums[: narrow_count * slot].reshape(LAYERS, len(narrow_list), slot)
    grad_fc_b = sums[narrow_count * slot : used].reshape(LAYERS, fc_slot)
    grad_w_qkv = jnp.stack([total for total in qkv_sums])
    grad_w_proj, grad_w_fc, grad_w_out = (
        jnp.stack([sums[n] for sums in other_sums]) for n in range(3)
    )
    return (
        output_rows,
        grad_rows,
        narrow_sums[:, 0],
        narrow_sums[:, 1],
        grad_w_qkv,
        narrow_sums[:, 2],
        narrow_sums[:, 3],
        grad_w_out,
        narrow_sums[:, 4],
        narrow_sums[:, 5],
        narrow_sums[:, 6],
        grad_w_fc,
        grad_fc_b,
        grad_w_proj,
        narrow_sums[:, 7],
    )


def solution(mesh):
    return jax.shard_map(
        shards,
        mesh=mesh,
        in_specs=(
            P("dp", "ctx", None),
            P("dp", "ctx"),
            P("dp", "ctx", None),
            P(None, ("dp", "ctx")),
            P(None, ("dp", "ctx")),
            P(None, ("dp", "ctx"), None),
            P(None, ("dp", "ctx")),
            P(None, ("dp", "ctx")),
            P(None, ("dp", "ctx"), None),
            P(None, ("dp", "ctx")),
            P(None, ("dp", "ctx")),
            P(None, ("dp", "ctx")),
            P(None, ("dp", "ctx"), None),
            P(None, ("dp", "ctx")),
            P(None, ("dp", "ctx"), None),
            P(None, ("dp", "ctx")),
        ),
        out_specs=(
            P("dp", "ctx", None),
            P("dp", "ctx", None),
            P(None, ("dp", "ctx")),
            P(None, ("dp", "ctx")),
            P(None, ("dp", "ctx"), None),
            P(None, ("dp", "ctx")),
            P(None, ("dp", "ctx")),
            P(None, ("dp", "ctx"), None),
            P(None, ("dp", "ctx")),
            P(None, ("dp", "ctx")),
            P(None, ("dp", "ctx")),
            P(None, ("dp", "ctx"), None),
            P(None, ("dp", "ctx")),
            P(None, ("dp", "ctx"), None),
            P(None, ("dp", "ctx")),
        ),
        check_vma=False,
    )
```
